512 devices in a mesh: leaf: 256 (over x, z, y), probe: 2 (over core).
Axes of the slice: x: 4, y: 8, z: 8, core: 2. Of those that a mesh axis runs over, the one named last changes fastest.
Arguments:
- features: bfloat16 [8, 786432], P(None, 'leaf'), may hold values from -5 to 5
- probes: bfloat16 [256, 786432], P('probe', 'leaf'), may hold values from -6 to 6
- lengthscale: float32 [8], replicated, may hold values from 1 to 4
- near_blocks: int32 [3072, 10], P('leaf'), may hold values from 0 to 3071, as said below
- leaf_order: int32 [256, 3072], P('leaf'), may hold values from 0 to 3071, each once within a row
Outputs:
- transfer: float32 [4, 65536, 256], P(None, 'leaf', 'probe')
- basis: float32 [786432, 256], P('leaf', 'probe')
The draws below stay inside these ranges and needn't reach their ends.
Inputs may be any that keep to these rules, and one draw needn't show every extreme that they name: `near_blocks`: row a lists 10 distinct blocks, its first entry is a itself, and all belong to leaves a // 12 - 1 to a // 12 + 1. `leaf_order`: each row is a permutation.
All inputs are finite; a program needn't handle non-finite values.
Results may differ from the reference program's by a relative error of at most 0.0053.
Values may be sent and summed in bfloat16 or wider, within the bound.
No kernel may reach another device: no remote copies, remote signals or barrier semaphores. Data moves between devices by JAX's collectives and lax.ppermute only.
A program may use at most 128 MiB of HBM per device.

```python
import math
import jax
import jax.numpy as jnp
from jax import lax

FEATS = 8
RANK = 256
BLOCK = 256
BLK_DEV = 12
NEAR = 10
LEVELS = 4
LEAF = 3072
BLOCKS = 3072
DESIGNS = 786432
GROUP = 16
N_LEAF = 256


def draw_near_blocks(key, part):
    count = 3 * BLK_DEV
    row_ids = jnp.arange(BLOCKS, dtype=jnp.int32)[:, None]
    slots = jnp.arange(count, dtype=jnp.int32)[None, :]
    home = row_ids // BLK_DEV
    global_ids = (home - 1) * BLK_DEV + slots
    valid = (global_ids >= 0) & (global_ids < BLOCKS)
    scores = jax.random.randint(key, (BLOCKS, count), 0, 1048576, dtype=jnp.int32) * count + slots
    scores = jnp.where(valid, scores, 1073741824)
    scores = jnp.where(global_ids == row_ids, -1, scores)
    picked = jnp.argsort(scores, axis=1, stable=True)[:, :NEAR]
    return jnp.take_along_axis(global_ids, picked, axis=1).astype(jnp.int32)


def levels(stream_key, shape, cuts, least, high):
    gain = 1.0
    for position, parts in cuts:
        draws = jax.random.uniform(jax.random.fold_in(jax.random.fold_in(stream_key, 6), position), (parts,), jnp.float32, least / len(cuts), high / len(cuts))
        gain = gain * jnp.repeat(jnp.exp(draws), shape[position] // parts).reshape((-1,) + (1,) * (len(shape) - 1 - position))
    return gain


def gaussian(key, extent, width, limit, cuts=(), kind=jnp.bfloat16):
    entries = width * jax.random.normal(key, extent, jnp.float32)
    if cuts:
        entries = entries * levels(key, extent, cuts, -0.22, 0.18)
    return jnp.clip(entries, -limit, limit).astype(kind)


def setup_inputs(seed: int = 0) -> dict:
    keys = jax.random.split(jax.random.key(seed), 6)
    features = gaussian(keys[0], (FEATS, DESIGNS), 1.0, 5.0, ((1, 256),))
    probes = gaussian(keys[1], (RANK, DESIGNS), 1.0, 6.0, ((0, 2), (1, 256)))
    lengthscale = jnp.clip(jnp.exp(jax.random.uniform(keys[2], (FEATS,), jnp.float32, math.log(1.0), math.log(4.0))), 1.0, 4.0)
    near_blocks = draw_near_blocks(jax.random.fold_in(keys[5], 71), 0)
    leaf_order = jax.vmap(lambda own: jax.random.permutation(own, LEAF))(jax.random.split(keys[4], N_LEAF)).reshape((N_LEAF, LEAF)).astype(jnp.int32)
    return dict(features=features, probes=probes, lengthscale=lengthscale, near_blocks=near_blocks, leaf_order=leaf_order)


root_three = 1.7320508075688772
nugget_var = 2.0

def lower_solve(lower, right):
    return lax.linalg.triangular_solve(lower, right, left_side=True, lower=True)

def kernel_tile(row_feat, col_feat, lengthscale):
    dist_sq = jnp.zeros((row_feat.shape[1],) + col_feat.shape[1:], jnp.float32)
    for feature in range(row_feat.shape[0]):
        diff = (row_feat[feature][:, None, None] - col_feat[feature][None]) / lengthscale[feature]
        dist_sq = dist_sq + diff * diff
    scaled = root_three * jnp.sqrt(dist_sq)
    return ((1.0 + scaled) * jnp.exp(-scaled)).astype(jnp.bfloat16)

def reference(features, probes, lengthscale, near_blocks, leaf_order):
    offsets = (jnp.arange(N_LEAF, dtype=jnp.int32)[:, None] * LEAF).astype(jnp.int32)
    index = (offsets + leaf_order.astype(jnp.int32)).reshape(-1).astype(jnp.int32)
    ordered = features[:, index]
    feat_blocks = ordered.astype(jnp.float32).reshape(FEATS, BLOCKS, BLOCK)
    probe_blocks = probes.reshape(RANK, BLOCKS, BLOCK)

    def one_block(start):
        listed = near_blocks[start]
        kern = kernel_tile(feat_blocks[:, start], feat_blocks[:, listed], lengthscale)
        columns = probe_blocks[:, listed].astype(jnp.float32)
        total = jnp.einsum('ucv,rcv->ur', kern.astype(jnp.float32), columns)
        return total + nugget_var * probe_blocks[:, start].astype(jnp.float32).T
    sketch = lax.map(one_block, jnp.arange(BLOCKS, dtype=jnp.int32))
    sketch = sketch.reshape(N_LEAF, LEAF, RANK)
    gram = jnp.einsum('nlr,nls->nrs', sketch, sketch, precision=lax.Precision.HIGHEST)
    grams = [gram]
    for depth in range(LEVELS):
        partner = jnp.arange(N_LEAF, dtype=jnp.int32) ^ 1 << depth
        gram = gram + gram[partner]
        grams.append(gram)
    factors = [jnp.linalg.cholesky(item) for item in grams]
    solver = jax.vmap(lower_solve)
    pieces = []
    for depth in range(1, LEVELS + 1):
        mixed = solver(factors[depth], factors[depth - 1])
        pieces.append(jnp.swapaxes(mixed, 1, 2).reshape(N_LEAF * RANK, RANK))
    transfer = jnp.stack(pieces, 0)
    solved = solver(factors[LEVELS], jnp.swapaxes(sketch, 1, 2))
    basis = jnp.swapaxes(solved, 1, 2).reshape(DESIGNS, RANK) * math.sqrt(GROUP * LEAF)
    return (transfer, basis)
```

```python
import math

import jax
import jax.numpy as jnp
from jax import lax
from jax.experimental import pallas as pl
from jax.experimental.pallas import tpu as pltpu
from jax.sharding import PartitionSpec as P

LEVELS = 4
LANES = 128
ROWS = 8
LOG2_E = 1.4426950408889634
LN_2 = 0.6931471805599453
NUGGET = 2.0
TINY = 1e-20
HI = lax.Precision.HIGHEST
F32 = jnp.float32
BF16 = jnp.bfloat16
VMEM_BYTES = 48 << 20


def call(kernel, out_shape, **kwargs):
    return pl.pallas_call(
        kernel,
        out_shape=out_shape,
        compiler_params=pltpu.CompilerParams(vmem_limit_bytes=VMEM_BYTES),
        **kwargs,
    )


def dot(a, b, ca, cb, precision=HI):
    return lax.dot_general(
        a, b, (((ca,), (cb,)), ((), ())), precision=precision, preferred_element_type=F32
    )


def dot16(a, b, ca, cb):
    return lax.dot_general(a, b, (((ca,), (cb,)), ((), ())), preferred_element_type=F32)


def halves(x):
    hi = x.astype(BF16)
    return hi, (x - hi.astype(F32)).astype(BF16)


def thirds(x):
    hi = x.astype(BF16).astype(F32)
    rest = x - hi
    mid = rest.astype(BF16).astype(F32)
    return hi, mid, rest - mid


def order_kernel(feat, order, out):
    chunks = feat.shape[1] // LANES
    pieces = [feat[:, c * LANES : (c + 1) * LANES].astype(F32) for c in range(chunks)]

    def one(q, carry):
        at = pl.multiple_of(q * LANES, LANES)
        index = jnp.broadcast_to(order[:, pl.ds(at, LANES)], (ROWS, LANES))
        low, high = index & (LANES - 1), index >> 7
        total = jnp.zeros((ROWS, LANES), F32)
        for c in range(chunks):
            total = jnp.where(high == c, jnp.take_along_axis(pieces[c], low, axis=1), total)
        out[:, pl.ds(at, LANES)] = total.astype(BF16)
        return carry

    lax.fori_loop(0, chunks, one, 0)


def order_features(features, leaf_order):
    return call(order_kernel, jax.ShapeDtypeStruct(features.shape, BF16))(features, leaf_order)


def tile_kernel(ids, own, left, right, scale, out, rows_t, cols):
    step = pl.program_id(0)
    leaf = own.shape[1]
    near = ids.shape[1]
    block = rows_t.shape[0] // pl.num_programs(0)

    @pl.when(step == 0)
    def _():
        weight = (3.0 * LOG2_E * LOG2_E) / (scale[...] * scale[...])
        for n, ref in enumerate((left, own, right)):
            x = ref[...].astype(F32)
            norm = jnp.sum(x * x * weight, 0, keepdims=True)
            norms = thirds(norm)
            ones = jnp.ones_like(norm)
            zeros = jnp.zeros((2, leaf), F32)
            cols[:, n * leaf : (n + 1) * leaf] = jnp.concatenate(
                [x, x, x, *norms, ones, ones, ones, zeros], 0
            ).astype(BF16)
            if n == 1:
                parts = thirds(-2.0 * weight * x)
                rows_t[...] = jnp.concatenate(
                    [*parts, ones, ones, ones, *norms, zeros], 0
                ).T.astype(BF16)

    mine = rows_t[pl.ds(pl.multiple_of(step * block, block), block), :]
    for j in range(near):
        at = pl.multiple_of(ids[step, j] * block, block)
        dist = dot16(mine, cols[:, pl.ds(at, block)], 1, 0)
        dist = jnp.maximum(dist, TINY)
        root = dist * lax.rsqrt(dist)
        kern = (1.0 + LN_2 * root) * jnp.exp2(-root)
        if j == 0:
            here = lax.broadcasted_iota(jnp.int32, (block, block), 0)
            there = lax.broadcasted_iota(jnp.int32, (block, block), 1)
            kern = jnp.where(here == there, kern + NUGGET, kern)
        out[0, :, j * block : (j + 1) * block] = kern.astype(BF16)


def kernel_tiles(ids, own, left, right, scale):
    leaf = own.shape[1]
    blocks, near = ids.shape
    block = leaf // blocks
    whole = pl.BlockSpec(memory_space=pltpu.VMEM)
    return call(
        tile_kernel,
        jax.ShapeDtypeStruct((blocks, block, near * block), BF16),
        grid_spec=pltpu.PrefetchScalarGridSpec(
            num_scalar_prefetch=1,
            grid=(blocks,),
            in_specs=[whole] * 4,
            out_specs=pl.BlockSpec((1, block, near * block), lambda i, ids: (i, 0, 0)),
            scratch_shapes=[pltpu.VMEM((leaf, 32), BF16), pltpu.VMEM((32, 3 * leaf), BF16)],
        ),
    )(ids, own, left, right, scale)


def sketch_kernel(ids, tiles, left, own, right, out, panel):
    step = pl.program_id(0)
    near = ids.shape[1]
    leaf = own.shape[1]
    block = tiles.shape[1]

    @pl.when(step == 0)
    def _():
        for n, ref in enumerate((left, own, right)):
            panel[:, n * leaf : (n + 1) * leaf] = ref[...]

    total = jnp.zeros(out.shape, F32)
    for j in range(near):
        at = pl.multiple_of(ids[step, j] * block, block)
        total += dot16(tiles[0, :, j * block : (j + 1) * block], panel[:, pl.ds(at, block)], 1, 1)
    out[...] = total


def sketch_rows(ids, tiles, left, own, right):
    half, leaf = own.shape
    blocks, block, width = tiles.shape
    whole = pl.BlockSpec(memory_space=pltpu.VMEM)
    return call(
        sketch_kernel,
        jax.ShapeDtypeStruct((leaf, half), F32),
        grid_spec=pltpu.PrefetchScalarGridSpec(
            num_scalar_prefetch=1,
            grid=(blocks,),
            in_specs=[pl.BlockSpec((1, block, width), lambda i, ids: (i, 0, 0))] + [whole] * 3,
            out_specs=pl.BlockSpec((block, half), lambda i, ids: (i, 0)),
            scratch_shapes=[pltpu.VMEM((half, 3 * leaf), BF16)],
        ),
    )(ids, tiles, left, own, right)


def gram_kernel(me, own, other, out):
    @pl.when(pl.program_id(0) == 0)
    def _():
        out[...] = jnp.zeros_like(out)

    def add(first, second):
        a0, a1 = halves(first)
        b0, b1 = halves(second)
        n = a0.shape[1]
        out[0:n] += dot16(a0, a0, 0, 0) + (dot16(a0, a1, 0, 0) + dot16(a1, a0, 0, 0))
        out[n : 2 * n] += dot16(b0, a0, 0, 0) + (dot16(b0, a1, 0, 0) + dot16(b1, a0, 0, 0))
        out[2 * n :] += dot16(b0, b0, 0, 0) + (dot16(b0, b1, 0, 0) + dot16(b1, b0, 0, 0))

    @pl.when(me[0] == 0)
    def _():
        add(own[...], other[...])

    @pl.when(me[0] == 1)
    def _():
        add(other[...], own[...])


def gram_blocks(me, own, other):
    leaf, half = own.shape
    steps = 4
    rows = pl.BlockSpec((leaf // steps, half), lambda i, me: (i, 0))
    return call(
        gram_kernel,
        jax.ShapeDtypeStruct((3 * half, half), F32),
        grid_spec=pltpu.PrefetchScalarGridSpec(
            num_scalar_prefetch=1,
            grid=(steps,),
            in_specs=[rows, rows],
            out_specs=pl.BlockSpec((3 * half, half), lambda i, me: (0, 0)),
        ),
    )(me, own, other)


def outer_sum(a, b):
    a0, a1, a2 = thirds(a)
    b0, b1, b2 = thirds(b)
    left = jnp.concatenate([a0, a0, a1, a0, a1, a2], 0).astype(BF16)
    right = jnp.concatenate([b0, b1, b0, b2, b1, b0], 0).astype(BF16)
    return dot16(left, right, 0, 0)


def eliminate(panels, units, diags):
    count = range(len(panels))
    tile = (ROWS, LANES)
    full = [[[None] * ROWS for _ in range(ROWS)] for _ in count]
    for m in range(ROWS):
        cols = [jnp.broadcast_to(diags[l][:, m : m + 1], tile) for l in count]
        for i in range(m, ROWS):
            for l in count:
                full[l][i][m] = jnp.broadcast_to(cols[l][i : i + 1, :], tile)
    rows = [[jnp.broadcast_to(panels[l][i : i + 1, :], tile) for i in range(ROWS)] for l in count]
    unit = [[jnp.broadcast_to(units[l][i : i + 1, :], tile) for i in range(ROWS)] for l in count]
    for k in range(ROWS):
        inv = [lax.rsqrt(full[l][k][k]) for l in count]
        low = [[None] * ROWS for _ in count]
        for i in range(k + 1, ROWS):
            for l in count:
                low[l][i] = full[l][i][k] * inv[l]
        for j in range(k + 1, ROWS):
            for i in range(j, ROWS):
                for l in count:
                    full[l][i][j] = full[l][i][j] - low[l][i] * low[l][j]
        for l in count:
            rows[l][k] = rows[l][k] * inv[l]
            unit[l][k] = unit[l][k] * inv[l]
        for i in range(k + 1, ROWS):
            for l in count:
                rows[l][i] = rows[l][i] - low[l][i] * rows[l][k]
                unit[l][i] = unit[l][i] - low[l][i] * unit[l][k]
    sub = lax.broadcasted_iota(jnp.int32, tile, 0)
    outs, invs = [], []
    for l in count:
        out, inv = rows[l][0], unit[l][0]
        for i in range(1, ROWS):
            out = jnp.where(sub == i, rows[l][i], out)
            inv = jnp.where(sub == i, unit[l][i], inv)
        outs.append(out)
        invs.append(inv)
    return outs, invs


def factor_block(work, ups, invs, base):
    count = range(work.shape[0])
    tile = (ROWS, LANES)
    lane = lax.broadcasted_iota(jnp.int32, tile, 1)
    sub = lax.broadcasted_iota(jnp.int32, tile, 0)
    lane_all = lax.broadcasted_iota(jnp.int32, (LANES, LANES), 1)
    span = slice(base, base + LANES)

    def step(j, carry):
        at = pl.multiple_of(j * ROWS, ROWS)
        here = (lane >= at) & (lane < at + ROWS)
        unit = jnp.where(lane - at == sub, 1.0, 0.0)
        panels = [work[l, pl.ds(at, ROWS), :] for l in count]
        diags = [pltpu.roll(panel, LANES - at, 1) for panel in panels]
        outs, units = eliminate(panels, [unit] * len(panels), diags)
        fulls = [jnp.where(here, units[l], outs[l]) for l in count]
        lefts = [jnp.where(lane >= at + ROWS, outs[l], 0.0) for l in count]
        sums = [outer_sum(lefts[l], fulls[l]) for l in count]
        gone = (lane_all >= at) & (lane_all < at + ROWS)
        rests = [jnp.where(gone, 0.0, work[l]) - sums[l] for l in count]
        for l in count:
            ups[l, pl.ds(base + at, ROWS), span] = jnp.where(lane >= at, outs[l], 0.0)
            invs[l, pl.ds(base + at, ROWS), span] = jnp.where(lane < at + ROWS, fulls[l], 0.0)
            work[l] = rests[l]
        return carry

    lax.fori_loop(0, LANES // ROWS, step, 0)


def factor(grams, work, ups, invs):
    n = LANES
    blank = jnp.zeros((n, n), F32)
    count = range(work.shape[0])
    for l in count:
        work[l] = grams(l, 0)
    factor_block(work, ups, invs, 0)
    for l in count:
        side = dot(invs[l, 0:n, 0:n], grams(l, 1), 1, 1)
        ups[l, 0:n, n : 2 * n] = side
        ups[l, n : 2 * n, 0:n] = blank
        invs[l, 0:n, n : 2 * n] = blank
        work[l] = grams(l, 2) - dot(side, side, 0, 0)
    factor_block(work, ups, invs, n)
    for l in count:
        down = dot(ups[l, 0:n, n : 2 * n], invs[l, 0:n, 0:n], 0, 0)
        invs[l, n : 2 * n, 0:n] = -dot(invs[l, n : 2 * n, n : 2 * n], down, 1, 0)


def factor_kernel(me, *refs):
    count = LEVELS + 1
    grams, (transfer, weight, work, ups, invs) = refs[:count], refs[count:]
    factor(lambda l, b: grams[l][b * LANES : (b + 1) * LANES, :], work, ups, invs)
    cols = pl.ds(pl.multiple_of(me[0] * LANES, LANES), LANES)
    for l in range(LEVELS):
        transfer[l] = dot(ups[l], invs[l + 1, cols, :], 1, 1)
    weight[...] = invs[LEVELS, cols, :]


def factors(me, grams):
    n = 2 * LANES
    count = len(grams)
    whole = pl.BlockSpec(memory_space=pltpu.VMEM)
    return call(
        factor_kernel,
        (
            jax.ShapeDtypeStruct((LEVELS, n, LANES), F32),
            jax.ShapeDtypeStruct((LANES, n), F32),
        ),
        grid_spec=pltpu.PrefetchScalarGridSpec(
            num_scalar_prefetch=1,
            grid=(1,),
            in_specs=[whole] * count,
            out_specs=[whole] * 2,
            scratch_shapes=[
                pltpu.VMEM((count, LANES, LANES), F32),
                pltpu.VMEM((count, n, n), F32),
                pltpu.VMEM((count, n, n), F32),
            ],
        ),
    )(me, *grams)


def basis_kernel(me, own, other, weight, out):
    n = LANES
    scale = math.sqrt(2**LEVELS * own.shape[0] * pl.num_programs(0))
    mine = pl.ds(pl.multiple_of(me[0] * n, n), n)
    rest = pl.ds(pl.multiple_of((1 - me[0]) * n, n), n)
    total = None
    for ref, cols in ((own, mine), (other, rest)):
        a0, a1 = halves(ref[...])
        b0, b1 = halves(weight[:, cols] * scale)
        part = dot16(a0, b0, 1, 1) + (dot16(a0, b1, 1, 1) + dot16(a1, b0, 1, 1))
        total = part if total is None else total + part
    out[...] = total


def basis_rows(me, own, other, weight):
    leaf, half = own.shape
    steps = 4
    rows = pl.BlockSpec((leaf // steps, half), lambda i, me: (i, 0))
    return call(
        basis_kernel,
        jax.ShapeDtypeStruct((leaf, half), F32),
        grid_spec=pltpu.PrefetchScalarGridSpec(
            num_scalar_prefetch=1,
            grid=(steps,),
            in_specs=[rows, rows, pl.BlockSpec((half, 2 * half), lambda i, me: (0, 0))],
            out_specs=rows,
        ),
    )(me, own, other, weight)


def beside(array, shift):
    count = lax.axis_size("leaf")
    pairs = [(i, i + shift) for i in range(count) if 0 <= i + shift < count]
    return lax.ppermute(array, "leaf", pairs)


def sibling(array, bit):
    return lax.ppermute(array, "leaf", [(i, i ^ 1 << bit) for i in range(lax.axis_size("leaf"))])


def other_core(array):
    return lax.ppermute(array, "probe", [(0, 1), (1, 0)])


def body(features, probes, lengthscale, near_blocks, leaf_order):
    blocks = near_blocks.shape[0]
    me = lax.axis_index("probe").astype(jnp.int32)[None]
    ids = near_blocks - (lax.axis_index("leaf") - 1) * blocks
    ordered = order_features(features, leaf_order)
    before = beside(ordered, 1)
    after = beside(ordered, -1)
    probes_before = beside(probes, 1)
    probes_after = beside(probes, -1)
    tiles = kernel_tiles(ids, ordered, before, after, lengthscale[:, None])
    own = sketch_rows(ids, tiles, probes_before, probes, probes_after)
    other = other_core(own)
    gram = gram_blocks(me, own, other)
    grams = [gram]
    for depth in range(LEVELS):
        gram = gram + sibling(gram, depth)
        grams.append(gram)
    transfer, weight = factors(me, grams)
    basis = basis_rows(me, own, other, weight)
    return transfer, basis


def solution(mesh):
    in_specs = (P(None, "leaf"), P("probe", "leaf"), P(), P("leaf", None), P("leaf", None))
    out_specs = (P(None, "leaf", "probe"), P("leaf", "probe"))
    return jax.shard_map(body, mesh=mesh, in_specs=in_specs, out_specs=out_specs, check_vma=False)
```

```python
import math

import jax
import jax.numpy as jnp
from jax import lax
from jax.experimental import pallas as pl
from jax.experimental.pallas import tpu as pltpu
from jax.sharding import PartitionSpec as P

LEVELS = 4
LANES = 128
ROWS = 8
LOG2_E = 1.4426950408889634
LN_2 = 0.6931471805599453
NUGGET = 2.0
TINY = 1e-20
HI = lax.Precision.HIGHEST
F32 = jnp.float32
BF16 = jnp.bfloat16
VMEM_BYTES = 14 << 20


def call(kernel, out_shape, **kwargs):
    return pl.pallas_call(
        kernel,
        out_shape=out_shape,
        compiler_params=pltpu.CompilerParams(vmem_limit_bytes=VMEM_BYTES),
        **kwargs,
    )


def dot(a, b, ca, cb, precision=HI):
    return lax.dot_general(
        a, b, (((ca,), (cb,)), ((), ())), precision=precision, preferred_element_type=F32
    )


def dot16(a, b, ca, cb):
    return lax.dot_general(a, b, (((ca,), (cb,)), ((), ())), preferred_element_type=F32)


def halves(x):
    hi = x.astype(BF16)
    return hi, (x - hi.astype(F32)).astype(BF16)


def thirds(x):
    hi = x.astype(BF16).astype(F32)
    rest = x - hi
    mid = rest.astype(BF16).astype(F32)
    return hi, mid, rest - mid


def order_kernel(feat, order, out):
    chunks = feat.shape[1] // LANES
    pieces = [feat[:, c * LANES : (c + 1) * LANES].astype(F32) for c in range(chunks)]

    def one(q, carry):
        at = pl.multiple_of(q * LANES, LANES)
        index = jnp.broadcast_to(order[:, pl.ds(at, LANES)], (ROWS, LANES))
        low, high = index & (LANES - 1), index >> 7
        total = jnp.zeros((ROWS, LANES), F32)
        for c in range(chunks):
            total = jnp.where(high == c, jnp.take_along_axis(pieces[c], low, axis=1), total)
        out[:, pl.ds(at, LANES)] = total.astype(BF16)
        return carry

    lax.fori_loop(0, chunks, one, 0)


def order_features(features, leaf_order):
    return call(order_kernel, jax.ShapeDtypeStruct(features.shape, BF16))(features, leaf_order)


SHIFT = 6
SLOTS = 128
WIDE = 4


def column_pieces(x, weight):
    norm = jnp.sum(x * x * weight, 0, keepdims=True)
    ones = jnp.ones_like(norm)
    zeros = jnp.zeros((2, x.shape[1]), F32)
    return jnp.concatenate([x, x, x, *thirds(norm), ones, ones, ones, zeros], 0).astype(BF16)


def row_pieces(x, weight):
    norm = jnp.sum(x * x * weight, 0, keepdims=True)
    ones = jnp.ones_like(norm)
    zeros = jnp.zeros((2, x.shape[1]), F32)
    return jnp.concatenate(
        [*thirds(-2.0 * weight * x), ones, ones, ones, *thirds(norm), zeros], 0
    ).T.astype(BF16)


def weights(scale):
    return (3.0 * LOG2_E * LOG2_E) / (scale[...] * scale[...])


def load_columns(cols, panel, feats, probes, weight, blocks):
    leaf = feats[0].shape[1]
    block = leaf // blocks
    for n, (feat, probe) in enumerate(zip(feats, probes)):
        pieces = column_pieces(feat[...].astype(F32), weight)
        for b in range(blocks):
            span = slice(b * block, (b + 1) * block)
            cols[n * blocks + b] = pieces[:, span]
            panel[n * blocks + b] = probe[:, span]
    last = len(feats) * blocks
    cols[last] = jnp.zeros(cols.shape[1:], BF16)
    panel[last] = jnp.zeros(panel.shape[1:], BF16)


def run_tasks(tasks, count, slot_of, rows_t, cols, panel, out):
    block = cols.shape[2]

    def some(t, carry):
        parts = []
        for u in range(WIDE):
            code = tasks[t * WIDE + u]
            at = pl.ds(pl.multiple_of((code >> SHIFT) * block, block), block)
            slot = slot_of(code & ((1 << SHIFT) - 1))
            dist = jnp.maximum(dot16(rows_t[at, :], cols[slot], 1, 0), TINY)
            root = dist * lax.rsqrt(dist)
            kern = (1.0 + LN_2 * root) * jnp.exp2(-root)
            parts.append((at, dot16(kern.astype(BF16), panel[slot], 1, 1)))
        for at, part in parts:
            out[at, :] += part
        return carry

    lax.fori_loop(0, (count + (WIDE - 1)) // WIDE, some, 0)


def near_kernel(ids, feat, scale, probes, out, rows_t, far, tasks, cols, panel):
    blocks, near = ids.shape
    block = feat.shape[1] // blocks

    def scan(a, counts):
        mine, rest = counts
        for j in range(near):
            listed = ids[a, j]
            code = (a << SHIFT) + listed
            inside = jnp.where((listed >= blocks) & (listed < 2 * blocks), 1, 0)
            tasks[mine] = code
            far[rest] = code
            mine = mine + inside
            rest = rest + (1 - inside)
        return mine, rest

    mine, rest = lax.fori_loop(0, blocks, scan, (jnp.int32(0), jnp.int32(0)))
    for u in range(WIDE):
        tasks[mine + u] = 2 * blocks
        far[rest + u] = 3 * blocks
    far[SLOTS - 1] = rest

    weight = weights(scale)
    rows_t[...] = row_pieces(feat[...].astype(F32), weight)
    load_columns(cols, panel, [feat], [probes], weight, blocks)
    here = lax.broadcasted_iota(jnp.int32, (block, block), 0)
    there = lax.broadcasted_iota(jnp.int32, (block, block), 1)
    nugget = jnp.where(here == there, NUGGET, 0.0).astype(BF16)
    for b in range(blocks):
        out[b * block : (b + 1) * block, :] = dot16(nugget, panel[b], 1, 1)
    run_tasks(tasks, mine, lambda listed: listed - blocks, rows_t, cols, panel, out)


def near_part(ids, feat, scale, probes):
    half, leaf = probes.shape
    blocks = ids.shape[0]
    block = leaf // blocks
    whole = pl.BlockSpec(memory_space=pltpu.VMEM)
    return call(
        near_kernel,
        (
            pltpu.VMEM((leaf, half), F32),
            pltpu.VMEM((leaf, 32), BF16),
            jax.ShapeDtypeStruct((SLOTS,), jnp.int32),
        ),
        grid_spec=pltpu.PrefetchScalarGridSpec(
            num_scalar_prefetch=1,
            grid=(1,),
            in_specs=[whole] * 3,
            out_specs=[whole, whole, pl.BlockSpec(memory_space=pltpu.SMEM)],
            scratch_shapes=[
                pltpu.SMEM((SLOTS,), jnp.int32),
                pltpu.VMEM((blocks + 1, 32, block), BF16),
                pltpu.VMEM((blocks + 1, half, block), BF16),
            ],
        ),
    )(ids, feat, scale, probes)


def far_kernel(far, part, rows_t, left, right, scale, before, after, out, cols, panel):
    blocks = (cols.shape[0] - 1) // 2
    load_columns(cols, panel, [left, right], [before, after], weights(scale), blocks)
    out[...] = part[...]
    run_tasks(
        far,
        far[SLOTS - 1],
        lambda listed: jnp.where(listed < blocks, listed, listed - blocks),
        rows_t,
        cols,
        panel,
        out,
    )


def far_part(far, part, rows_t, left, right, scale, before, after, blocks):
    half, leaf = before.shape
    block = leaf // blocks
    whole = pl.BlockSpec(memory_space=pltpu.VMEM)
    return call(
        far_kernel,
        pltpu.VMEM((leaf, half), F32),
        grid_spec=pltpu.PrefetchScalarGridSpec(
            num_scalar_prefetch=1,
            grid=(1,),
            in_specs=[whole] * 7,
            out_specs=whole,
            scratch_shapes=[
                pltpu.VMEM((2 * blocks + 1, 32, block), BF16),
                pltpu.VMEM((2 * blocks + 1, half, block), BF16),
            ],
        ),
    )(far, part, rows_t, left, right, scale, before, after)


def gram_kernel(me, own, other, out):
    n = own.shape[1]

    @pl.when(pl.program_id(0) == 0)
    def _():
        out[...] = jnp.zeros_like(out)

    def product(a, b):
        return dot16(a[0], b[0], 0, 0) + (dot16(a[0], b[1], 0, 0) + dot16(a[1], b[0], 0, 0))

    mine = halves(own[...])
    out[0:n] += product(mine, mine)

    @pl.when(me[0] == 0)
    def _():
        out[n:] += product(halves(other[:, : n // 2]), halves(own[...]))

    @pl.when(me[0] == 1)
    def _():
        out[n:] += product(halves(own[:, n // 2 :]), halves(other[...]))


def gram_blocks(me, own, other):
    leaf, half = own.shape
    steps = 4
    height = half + half // 2
    rows = pl.BlockSpec((leaf // steps, half), lambda i, me: (i, 0))
    return call(
        gram_kernel,
        jax.ShapeDtypeStruct((height, half), F32),
        grid_spec=pltpu.PrefetchScalarGridSpec(
            num_scalar_prefetch=1,
            grid=(steps,),
            in_specs=[rows, rows],
            out_specs=pl.BlockSpec((height, half), lambda i, me: (0, 0)),
        ),
    )(me, own, other)


TILE = (ROWS, LANES)


def row_of(x, k):
    return jnp.broadcast_to(x[k : k + 1, :], TILE)


def columns(panel, at):
    return [
        jnp.take_along_axis(panel, jnp.full(TILE, at + m, jnp.int32), axis=1)
        for m in range(ROWS)
    ]


def outer_sum(a, b):
    a0, a1, a2 = thirds(a)
    b0, b1, b2 = thirds(b)
    left = jnp.concatenate([a0, a0, a1, a0, a1, a2], 0).astype(BF16)
    right = jnp.concatenate([b0, b1, b0, b2, b1, b0], 0).astype(BF16)
    return dot16(left, right, 0, 0)


def eliminate(panels, nexts, at):
    count = range(len(panels))
    lane = lax.broadcasted_iota(jnp.int32, TILE, 1)
    sub = lax.broadcasted_iota(jnp.int32, TILE, 0)
    here = (lane >= at) & (lane < at + ROWS)
    unit = jnp.where(lane - at == sub, 1.0, 0.0)
    cols = [columns(panels[l], at) for l in count]
    rows = [jnp.where(here, unit, panels[l]) for l in count]
    lows = [jnp.zeros(TILE, F32) for l in count]
    below = [columns(panel, at) for panel in nexts]
    nexts = [jnp.where(here, 0.0, panel) for panel in nexts]
    for k in range(ROWS):
        inv = [lax.rsqrt(row_of(cols[l][k], k)) for l in count]
        low = [jnp.where(sub >= k, cols[l][k] * inv[l], 0.0) for l in count]
        for l in count:
            lead = row_of(rows[l], k) * inv[l]
            rows[l] = jnp.where(sub == k, lead, rows[l] - low[l] * lead)
            lows[l] = jnp.where(lane == at + k, low[l], lows[l])
            if nexts:
                below[l][k] = below[l][k] * inv[l]
                nexts[l] = nexts[l] - below[l][k] * lead
        for m in range(k + 1, ROWS):
            for l in count:
                one = row_of(low[l], m)
                cols[l][m] = cols[l][m] - low[l] * one
                if nexts:
                    below[l][m] = below[l][m] - below[l][k] * one
    return rows, lows, nexts


def factor_block(work, ups, invs, base):
    count = range(work.shape[0])
    lane = lax.broadcasted_iota(jnp.int32, TILE, 1)
    lane_all = lax.broadcasted_iota(jnp.int32, (LANES, LANES), 1)
    span = slice(base, base + LANES)
    pair = 2 * ROWS

    def step(j, carry):
        at = pl.multiple_of(j * pair, pair)
        mid, end = at + ROWS, at + pair
        both = [work[l, pl.ds(at, pair), :] for l in count]
        first, low_first, second = eliminate(
            [b[:ROWS] for b in both], [b[ROWS:] for b in both], at
        )
        second, low_second, _ = eliminate(second, [], mid)
        lefts, rights = [], []
        for l in count:
            lefts.append(
                jnp.concatenate([jnp.where(lane >= end, x[l], 0.0) for x in (first, second)], 0)
            )
            rights.append(
                jnp.concatenate(
                    [jnp.where((lane >= mid) & (lane < end), 0.0, first[l]), second[l]], 0
                )
            )
        sums = [outer_sum(lefts[l], rights[l]) for l in count]
        gone = (lane_all >= at) & (lane_all < end)
        rests = [jnp.where(gone, 0.0, work[l]) - sums[l] for l in count]
        for l in count:
            for x, low, p in ((first, low_first, at), (second, low_second, mid)):
                to = pl.ds(pl.multiple_of(base + p, ROWS), ROWS)
                ups[l, to, span] = jnp.where(lane >= p + ROWS, x[l], low[l])
                invs[l, to, span] = jnp.where(lane < p + ROWS, x[l], 0.0)
            work[l] = rests[l]
        return carry

    lax.fori_loop(0, LANES // pair, step, 0)


def straighten(ups, l, base):
    n = LANES
    block = ups[l, base : base + n, base : base + n]
    row = lax.broadcasted_iota(jnp.int32, (n, n), 0)
    col = lax.broadcasted_iota(jnp.int32, (n, n), 1)
    ups[l, base : base + n, base : base + n] = jnp.where(row >> 3 == col >> 3, block.T, block)


def factor(grams, work, ups, invs):
    n = LANES
    blank = jnp.zeros((n, n), F32)
    count = range(work.shape[0])
    for l in count:
        work[l] = grams(l, 0)
    factor_block(work, ups, invs, 0)
    sides = [dot(invs[l, 0:n, 0:n], grams(l, 1), 1, 1) for l in count]
    for l in count:
        ups[l, 0:n, n : 2 * n] = sides[l]
        ups[l, n : 2 * n, 0:n] = blank
        invs[l, 0:n, n : 2 * n] = blank
    squares = [dot(sides[l], sides[l], 0, 0) for l in count]
    for l in count:
        work[l] = grams(l, 2) - squares[l]
    factor_block(work, ups, invs, n)
    downs = [dot(ups[l, 0:n, n : 2 * n], invs[l, 0:n, 0:n], 0, 0) for l in count]
    downs = [dot(invs[l, n : 2 * n, n : 2 * n], downs[l], 1, 0) for l in count]
    for l in count:
        invs[l, n : 2 * n, 0:n] = -downs[l]
        straighten(ups, l, 0)
        straighten(ups, l, n)


def factor_kernel(me, mine, theirs, transfer, weight, pieces, work, ups, invs):
    n = LANES
    height = n + n // 2
    pieces[me[0]] = mine[...]
    pieces[1 - me[0]] = theirs[...]

    def gram(l, b):
        at = l * height
        if b == 1:
            return jnp.concatenate([pieces[p, at + n : at + height, :] for p in range(2)], 0)
        return pieces[b // 2, at : at + n, :]

    factor(gram, work, ups, invs)
    cols = pl.ds(pl.multiple_of(me[0] * n, n), n)
    for l in range(LEVELS):
        transfer[l] = dot(ups[l], invs[l + 1, cols, :], 1, 1)
    weight[...] = invs[LEVELS, cols, :]


def factors(me, mine, theirs):
    n = 2 * LANES
    count = LEVELS + 1
    whole = pl.BlockSpec(memory_space=pltpu.VMEM)
    return call(
        factor_kernel,
        (
            jax.ShapeDtypeStruct((LEVELS, n, LANES), F32),
            jax.ShapeDtypeStruct((LANES, n), F32),
        ),
        grid_spec=pltpu.PrefetchScalarGridSpec(
            num_scalar_prefetch=1,
            grid=(1,),
            in_specs=[whole] * 2,
            out_specs=[whole] * 2,
            scratch_shapes=[
                pltpu.VMEM((2, *mine.shape), F32),
                pltpu.VMEM((count, LANES, LANES), F32),
                pltpu.VMEM((count, n, n), F32),
                pltpu.VMEM((count, n, n), F32),
            ],
        ),
    )(me, mine, theirs)


def basis_kernel(me, own, other, weight, out):
    n = LANES
    scale = math.sqrt(2**LEVELS * own.shape[0] * pl.num_programs(0))
    mine = pl.ds(pl.multiple_of(me[0] * n, n), n)
    rest = pl.ds(pl.multiple_of((1 - me[0]) * n, n), n)
    total = None
    for ref, cols in ((own, mine), (other, rest)):
        a0, a1 = halves(ref[...])
        b0, b1 = halves(weight[:, cols] * scale)
        part = dot16(a0, b0, 1, 1) + (dot16(a0, b1, 1, 1) + dot16(a1, b0, 1, 1))
        total = part if total is None else total + part
    out[...] = total


def basis_rows(me, own, other, weight):
    leaf, half = own.shape
    steps = 4
    rows = pl.BlockSpec((leaf // steps, half), lambda i, me: (i, 0))
    return call(
        basis_kernel,
        jax.ShapeDtypeStruct((leaf, half), F32),
        grid_spec=pltpu.PrefetchScalarGridSpec(
            num_scalar_prefetch=1,
            grid=(steps,),
            in_specs=[rows, rows, pl.BlockSpec((half, 2 * half), lambda i, me: (0, 0))],
            out_specs=rows,
        ),
    )(me, own, other, weight)


def beside(array, shift):
    count = lax.axis_size("leaf")
    pairs = [(i, i + shift) for i in range(count) if 0 <= i + shift < count]
    return lax.ppermute(array, "leaf", pairs)


def sibling(array, bit):
    return lax.ppermute(array, "leaf", [(i, i ^ 1 << bit) for i in range(lax.axis_size("leaf"))])


def other_core(array):
    return lax.ppermute(array, "probe", [(0, 1), (1, 0)])


def body(features, probes, lengthscale, near_blocks, leaf_order):
    blocks = near_blocks.shape[0]
    me = lax.axis_index("probe").astype(jnp.int32)[None]
    ids = near_blocks - (lax.axis_index("leaf") - 1) * blocks
    scale = lengthscale[:, None]
    probes_before = beside(probes, 1)
    probes_after = beside(probes, -1)
    ordered = order_features(features, leaf_order)
    before = beside(ordered, 1)
    after = beside(ordered, -1)
    part, rows_t, far = near_part(ids, ordered, scale, probes)
    own = far_part(far, part, rows_t, before, after, scale, probes_before, probes_after, blocks)
    other = other_core(own)
    gram = gram_blocks(me, own, other)
    grams = [gram]
    for depth in range(LEVELS):
        gram = gram + sibling(gram, depth)
        grams.append(gram)
    mine = jnp.concatenate(grams, 0)
    transfer, weight = factors(me, mine, other_core(mine))
    basis = basis_rows(me, own, other, weight)
    return transfer, basis


def solution(mesh):
    in_specs = (P(None, "leaf"), P("probe", "leaf"), P(), P("leaf", None), P("leaf", None))
    out_specs = (P(None, "leaf", "probe"), P("leaf", "probe"))
    return jax.shard_map(body, mesh=mesh, in_specs=in_specs, out_specs=out_specs, check_vma=False)
```

```python
import math

import jax
import jax.numpy as jnp
from jax import lax
from jax.experimental import pallas as pl
from jax.experimental.pallas import tpu as pltpu
from jax.sharding import PartitionSpec as P

LEVELS = 4
LANES = 128
ROWS = 8
TILE = (ROWS, LANES)
LOG2_E = 1.4426950408889634
LN_2 = 0.6931471805599453
NUGGET = 2.0
TINY = 1e-20
HI = lax.Precision.HIGHEST
F32 = jnp.float32
BF16 = jnp.bfloat16
VMEM_BYTES = 14 << 20


def call(kernel, out_shape, **kwargs):
    return pl.pallas_call(
        kernel,
        out_shape=out_shape,
        compiler_params=pltpu.CompilerParams(vmem_limit_bytes=VMEM_BYTES),
        **kwargs,
    )


def dot(a, b, ca, cb, precision=HI):
    return lax.dot_general(
        a, b, (((ca,), (cb,)), ((), ())), precision=precision, preferred_element_type=F32
    )


def dot16(a, b, ca, cb):
    return lax.dot_general(a, b, (((ca,), (cb,)), ((), ())), preferred_element_type=F32)


def halves(x):
    hi = x.astype(BF16)
    return hi, (x - hi.astype(F32)).astype(BF16)


def thirds(x):
    hi = x.astype(BF16).astype(F32)
    rest = x - hi
    mid = rest.astype(BF16).astype(F32)
    return hi, mid, rest - mid


def order_kernel(feat, order, out):
    chunks = feat.shape[1] // LANES
    pieces = [feat[:, c * LANES : (c + 1) * LANES].astype(F32) for c in range(chunks)]

    def one(q, carry):
        at = pl.multiple_of(q * LANES, LANES)
        index = jnp.broadcast_to(order[:, pl.ds(at, LANES)], (ROWS, LANES))
        low, high = index & (LANES - 1), index >> 7
        total = jnp.zeros((ROWS, LANES), F32)
        for c in range(chunks):
            total = jnp.where(high == c, jnp.take_along_axis(pieces[c], low, axis=1), total)
        out[:, pl.ds(at, LANES)] = total.astype(BF16)
        return carry

    lax.fori_loop(0, chunks, one, 0)


def order_features(features, leaf_order):
    return call(order_kernel, jax.ShapeDtypeStruct(features.shape, BF16))(features, leaf_order)


SHIFT = 6
SLOTS = 160
WIDE = 4


def column_pieces(x, weight):
    norm = jnp.sum(x * x * weight, 0, keepdims=True)
    ones = jnp.ones_like(norm)
    zeros = jnp.zeros((2, x.shape[1]), F32)
    return jnp.concatenate([x, x, x, *thirds(norm), ones, ones, ones, zeros], 0).astype(BF16)


def row_pieces(x, weight):
    norm = jnp.sum(x * x * weight, 0, keepdims=True)
    ones = jnp.ones_like(norm)
    zeros = jnp.zeros((2, x.shape[1]), F32)
    return jnp.concatenate(
        [*thirds(-2.0 * weight * x), ones, ones, ones, *thirds(norm), zeros], 0
    ).T.astype(BF16)


def weights(scale):
    count = scale.shape[0]
    row = lax.broadcasted_iota(jnp.int32, (count, 1), 0)
    held = jnp.full((count, 1), scale[0], F32)
    for f in range(1, count):
        held = jnp.where(row == f, scale[f], held)
    return (3.0 * LOG2_E * LOG2_E) / (held * held)


def load_columns(cols, panel, feats, probes, weight, blocks):
    leaf = feats[0].shape[1]
    block = leaf // blocks
    for n, (feat, probe) in enumerate(zip(feats, probes)):
        pieces = column_pieces(feat[...].astype(F32), weight)
        for b in range(blocks):
            span = slice(b * block, (b + 1) * block)
            cols[n * blocks + b] = pieces[:, span]
            panel[n * blocks + b] = probe[:, span]
    last = len(feats) * blocks
    cols[last] = jnp.zeros(cols.shape[1:], BF16)
    panel[last] = jnp.zeros(panel.shape[1:], BF16)


def run_tasks(tasks, count, slot_of, rows_t, cols, panel, out, kerns):
    block = cols.shape[2]

    def where_of(n):
        code = tasks[n]
        at = pl.ds(pl.multiple_of((code >> SHIFT) * block, block), block)
        return at, slot_of(code & ((1 << SHIFT) - 1))

    def product(n, kern):
        at, slot = where_of(n)
        return at, dot16(kern, panel[slot], 1, 1)

    def some(i, carry):
        for half in range(2):
            group = 2 * i + half
            last = jnp.maximum(group - 1, 0)
            for u in range(WIDE):
                to, part = product(last * WIDE + u, kerns[1 - half][u])
                at, slot = where_of(group * WIDE + u)
                dist = jnp.maximum(dot16(rows_t[at, :], cols[slot], 1, 0), TINY)
                root = dist * lax.rsqrt(dist)
                kerns[half][u] = ((1.0 + LN_2 * root) * jnp.exp2(-root)).astype(BF16)
                out[to, :] += part
        return carry

    kerns[1][...] = jnp.zeros_like(kerns[1])
    pairs = (count + (2 * WIDE - 1)) // (2 * WIDE)
    lax.fori_loop(0, pairs, some, 0)
    for u in range(WIDE):
        to, part = product(jnp.maximum(2 * pairs - 1, 0) * WIDE + u, kerns[1][u])
        out[to, :] += part


def near_kernel(near_blocks, first, scale, feat, probes, out, rows_t, far, tasks, cols, panel, k0, k1):
    blocks, near = near_blocks.shape
    block = feat.shape[1] // blocks

    def scan(a, counts):
        mine, rest = counts
        for j in range(near):
            listed = near_blocks[a, j] - first[0]
            code = (a << SHIFT) + listed
            inside = jnp.where((listed >= blocks) & (listed < 2 * blocks), 1, 0)
            tasks[mine] = code
            far[rest] = code
            mine = mine + inside
            rest = rest + (1 - inside)
        return mine, rest

    mine, rest = lax.fori_loop(0, blocks, scan, (jnp.int32(0), jnp.int32(0)))
    for u in range(2 * WIDE):
        tasks[mine + u] = 2 * blocks
        far[rest + u] = 3 * blocks
    far[SLOTS - 1] = rest

    weight = weights(scale)
    rows_t[...] = row_pieces(feat[...].astype(F32), weight)
    load_columns(cols, panel, [feat], [probes], weight, blocks)
    here = lax.broadcasted_iota(jnp.int32, (block, block), 0)
    there = lax.broadcasted_iota(jnp.int32, (block, block), 1)
    nugget = jnp.where(here == there, NUGGET, 0.0).astype(BF16)
    for b in range(blocks):
        out[b * block : (b + 1) * block, :] = dot16(nugget, panel[b], 1, 1)
    run_tasks(tasks, mine, lambda listed: listed - blocks, rows_t, cols, panel, out, (k0, k1))


def near_part(near_blocks, first, scale, feat, probes):
    half, leaf = probes.shape
    blocks = near_blocks.shape[0]
    block = leaf // blocks
    whole = pl.BlockSpec(memory_space=pltpu.VMEM)
    return call(
        near_kernel,
        (
            pltpu.VMEM((leaf, half), F32),
            pltpu.VMEM((leaf, 32), BF16),
            jax.ShapeDtypeStruct((SLOTS,), jnp.int32),
        ),
        grid_spec=pltpu.PrefetchScalarGridSpec(
            num_scalar_prefetch=3,
            grid=(1,),
            in_specs=[whole] * 2,
            out_specs=[whole, whole, pl.BlockSpec(memory_space=pltpu.SMEM)],
            scratch_shapes=[
                pltpu.SMEM((SLOTS,), jnp.int32),
                pltpu.VMEM((blocks + 1, 32, block), BF16),
                pltpu.VMEM((blocks + 1, half, block), BF16),
                *[pltpu.VMEM((WIDE, block, block), BF16)] * 2,
            ],
        ),
    )(near_blocks, first, scale, feat, probes)


def far_kernel(far, scale, part, rows_t, left, right, before, after, out, cols, panel, k0, k1):
    blocks = (cols.shape[0] - 1) // 2
    load_columns(cols, panel, [left, right], [before, after], weights(scale), blocks)
    out[...] = part[...]
    run_tasks(
        far,
        far[SLOTS - 1],
        lambda listed: jnp.where(listed < blocks, listed, listed - blocks),
        rows_t,
        cols,
        panel,
        out,
        (k0, k1),
    )


def far_part(far, scale, part, rows_t, left, right, before, after, blocks):
    half, leaf = before.shape
    block = leaf // blocks
    whole = pl.BlockSpec(memory_space=pltpu.VMEM)
    return call(
        far_kernel,
        pltpu.VMEM((leaf, half), F32),
        grid_spec=pltpu.PrefetchScalarGridSpec(
            num_scalar_prefetch=2,
            grid=(1,),
            in_specs=[whole] * 6,
            out_specs=whole,
            scratch_shapes=[
                pltpu.VMEM((2 * blocks + 1, 32, block), BF16),
                pltpu.VMEM((2 * blocks + 1, half, block), BF16),
                *[pltpu.VMEM((WIDE, block, block), BF16)] * 2,
            ],
        ),
    )(far, scale, part, rows_t, left, right, before, after)


HALF = LANES // 2
PACKED = HALF + ROWS


def pack(block):
    shape = (HALF, LANES)
    row = lax.broadcasted_iota(jnp.int32, shape, 0)
    col = lax.broadcasted_iota(jnp.int32, shape, 1) - HALF
    bottom = block[HALF:, :]
    top = pltpu.roll(block[:HALF, :], HALF, 1)
    diagonal = jnp.sum(jnp.where(row == col, bottom, 0.0), 0, keepdims=True)
    body = jnp.where((col >= 0) & (row >= col), top, bottom)
    return body, jnp.broadcast_to(diagonal, TILE)


def unpack(body, diagonal):
    shape = (HALF, HALF)
    row = lax.broadcasted_iota(jnp.int32, shape, 0)
    col = lax.broadcasted_iota(jnp.int32, shape, 1)
    side = body[:, :HALF]
    fold = body[:, HALF:]
    flip = fold.T
    top = jnp.where(row >= col, fold, flip)
    bottom = jnp.where(row < col, fold, flip)
    bottom = jnp.where(row == col, diagonal[:1, HALF:], bottom)
    return jnp.concatenate(
        [jnp.concatenate([top, side.T], 1), jnp.concatenate([side, bottom], 1)], 0
    )


def product(a, b):
    return dot16(a[0], b[0], 0, 0) + (dot16(a[0], b[1], 0, 0) + dot16(a[1], b[0], 0, 0))


def own_kernel(own, out, high, low):
    a0, a1 = halves(own[...])
    high[...] = a0
    low[...] = a1
    out[:HALF], out[HALF:] = pack(product((a0, a1), (a0, a1)))


def own_gram(own):
    leaf, half = own.shape
    return call(
        own_kernel,
        (
            pltpu.VMEM((PACKED, half), F32),
            pltpu.VMEM((leaf, half), BF16),
            pltpu.VMEM((leaf, half), BF16),
        ),
    )(own)


def gram_kernel(me, block, high, low, other, out, high_o, low_o):
    b0, b1 = halves(other[...])
    high_o[...] = b0
    low_o[...] = b1
    out[:PACKED] = block[...]

    @pl.when(me[0] == 0)
    def _():
        out[PACKED:] = product((b0[:, :HALF], b1[:, :HALF]), (high[...], low[...]))

    @pl.when(me[0] == 1)
    def _():
        out[PACKED:] = product((high[:, HALF:], low[:, HALF:]), (b0, b1))


def gram_blocks(me, block, high, low, other):
    leaf, half = other.shape
    whole = pl.BlockSpec(memory_space=pltpu.VMEM)
    return call(
        gram_kernel,
        (
            jax.ShapeDtypeStruct((PACKED + HALF, half), F32),
            pltpu.VMEM((leaf, half), BF16),
            pltpu.VMEM((leaf, half), BF16),
        ),
        grid_spec=pltpu.PrefetchScalarGridSpec(
            num_scalar_prefetch=1, grid=(1,), in_specs=[whole] * 4, out_specs=[whole] * 3
        ),
    )(me, block, high, low, other)


def row_of(x, k):
    return jnp.broadcast_to(x[k : k + 1, :], TILE)


def columns(panel, at):
    return [
        jnp.take_along_axis(panel, jnp.full(TILE, at + m, jnp.int32), axis=1)
        for m in range(ROWS)
    ]


def outer_sum(a, b):
    a0, a1, a2 = thirds(a)
    b0, b1, b2 = thirds(b)
    left = jnp.concatenate([a0, a0, a1, a0, a1, a2], 0).astype(BF16)
    right = jnp.concatenate([b0, b1, b0, b2, b1, b0], 0).astype(BF16)
    return dot16(left, right, 0, 0)


def eliminate(panels, nexts, at):
    count = range(len(panels))
    lane = lax.broadcasted_iota(jnp.int32, TILE, 1)
    sub = lax.broadcasted_iota(jnp.int32, TILE, 0)
    here = (lane >= at) & (lane < at + ROWS)
    unit = jnp.where(lane - at == sub, 1.0, 0.0)
    cols = [columns(panels[l], at) for l in count]
    rows = [jnp.where(here, unit, panels[l]) for l in count]
    lows = [jnp.zeros(TILE, F32) for l in count]
    below = [columns(panel, at) for panel in nexts]
    nexts = [jnp.where(here, 0.0, panel) for panel in nexts]
    for k in range(ROWS):
        inv = [lax.rsqrt(row_of(cols[l][k], k)) for l in count]
        low = [jnp.where(sub >= k, cols[l][k] * inv[l], 0.0) for l in count]
        for l in count:
            lead = row_of(rows[l], k) * inv[l]
            rows[l] = jnp.where(sub == k, lead, rows[l] - low[l] * lead)
            lows[l] = jnp.where(lane == at + k, low[l], lows[l])
            if nexts:
                below[l][k] = below[l][k] * inv[l]
                nexts[l] = nexts[l] - below[l][k] * lead
        for m in range(k + 1, ROWS):
            for l in count:
                one = row_of(low[l], m)
                cols[l][m] = cols[l][m] - low[l] * one
                if nexts:
                    below[l][m] = below[l][m] - below[l][k] * one
    return rows, lows, nexts


def factor_block(work, ups, invs, base):
    count = range(work.shape[0])
    lane = lax.broadcasted_iota(jnp.int32, TILE, 1)
    lane_all = lax.broadcasted_iota(jnp.int32, (LANES, LANES), 1)
    span = slice(base, base + LANES)
    pair = 2 * ROWS

    def step(j, carry):
        at = pl.multiple_of(j * pair, pair)
        mid, end = at + ROWS, at + pair
        both = [work[l, pl.ds(at, pair), :] for l in count]
        first, low_first, second = eliminate(
            [b[:ROWS] for b in both], [b[ROWS:] for b in both], at
        )
        second, low_second, _ = eliminate(second, [], mid)
        lefts, rights = [], []
        for l in count:
            lefts.append(
                jnp.concatenate([jnp.where(lane >= end, x[l], 0.0) for x in (first, second)], 0)
            )
            rights.append(
                jnp.concatenate(
                    [jnp.where((lane >= mid) & (lane < end), 0.0, first[l]), second[l]], 0
                )
            )
        sums = [outer_sum(lefts[l], rights[l]) for l in count]
        gone = (lane_all >= at) & (lane_all < end)
        rests = [jnp.where(gone, 0.0, work[l]) - sums[l] for l in count]
        for l in count:
            for x, low, p in ((first, low_first, at), (second, low_second, mid)):
                to = pl.ds(pl.multiple_of(base + p, ROWS), ROWS)
                ups[l, to, span] = jnp.where(lane >= p + ROWS, x[l], low[l])
                invs[l, to, span] = jnp.where(lane < p + ROWS, x[l], 0.0)
            work[l] = rests[l]
        return carry

    lax.fori_loop(0, LANES // pair, step, 0)


def straighten(ups, l, base):
    n = LANES
    block = ups[l, base : base + n, base : base + n]
    row = lax.broadcasted_iota(jnp.int32, (n, n), 0)
    col = lax.broadcasted_iota(jnp.int32, (n, n), 1)
    ups[l, base : base + n, base : base + n] = jnp.where(row >> 3 == col >> 3, block.T, block)


def factor(grams, work, ups, invs):
    n = LANES
    blank = jnp.zeros((n, n), F32)
    count = range(work.shape[0])
    for l in count:
        work[l] = grams(l, 0)
    factor_block(work, ups, invs, 0)
    sides = [dot(invs[l, 0:n, 0:n], grams(l, 1), 1, 1) for l in count]
    for l in count:
        ups[l, 0:n, n : 2 * n] = sides[l]
        ups[l, n : 2 * n, 0:n] = blank
        invs[l, 0:n, n : 2 * n] = blank
    squares = [dot(sides[l], sides[l], 0, 0) for l in count]
    for l in count:
        work[l] = grams(l, 2) - squares[l]
    factor_block(work, ups, invs, n)
    downs = [dot(ups[l, 0:n, n : 2 * n], invs[l, 0:n, 0:n], 0, 0) for l in count]
    downs = [dot(invs[l, n : 2 * n, n : 2 * n], downs[l], 1, 0) for l in count]
    for l in count:
        invs[l, n : 2 * n, 0:n] = -downs[l]
        straighten(ups, l, 0)
        straighten(ups, l, n)


def factor_kernel(me, mine, theirs, own0, own1, other0, other1, transfer, basis, pieces, work, ups, invs, moved, rows, sems):
    n = LANES
    height = PACKED + HALF
    pieces[me[0]] = mine[...]
    pieces[1 - me[0]] = theirs[...]

    def gram(l, b):
        at = l * height
        if b == 1:
            return jnp.concatenate([pieces[p, at + PACKED : at + height, :] for p in range(2)], 0)
        part = pieces.at[b // 2]
        return unpack(part[at : at + HALF, :], part[at + HALF : at + PACKED, :])

    factor(gram, work, ups, invs)
    cols = pl.ds(pl.multiple_of(me[0] * n, n), n)
    rest = pl.ds(pl.multiple_of((1 - me[0]) * n, n), n)
    scale = math.sqrt(2**LEVELS * own0.shape[0])
    weight = invs.at[LEVELS]
    near0, near1 = halves(weight[cols, cols] * scale)
    far0, far1 = halves(weight[cols, rest] * scale)
    steps, size, _ = rows.shape
    copies = []
    for s in range(steps):
        at = slice(s * size, (s + 1) * size)
        a0, a1, b0, b1 = own0[at, :], own1[at, :], other0[at, :], other1[at, :]
        small = dot16(a0, near1, 1, 1) + dot16(a1, near0, 1, 1)
        small += dot16(b0, far1, 1, 1) + dot16(b1, far0, 1, 1)
        rows[s] = small + (dot16(a0, near0, 1, 1) + dot16(b0, far0, 1, 1))
        copies.append(pltpu.make_async_copy(rows.at[s], basis.at[pl.ds(s * size, size)], sems.at[s]))
        copies[-1].start()
    for l in range(LEVELS):
        moved[l] = dot(ups[l], invs[l + 1, cols, :], 1, 1)
        copies.append(pltpu.make_async_copy(moved.at[l], transfer.at[l], sems.at[steps + l]))
        copies[-1].start()
    for copy in copies:
        copy.wait()


def factors(me, mine, theirs, own, other):
    n = 2 * LANES
    count = LEVELS + 1
    leaf, half = own[0].shape
    steps = 6
    whole = pl.BlockSpec(memory_space=pltpu.VMEM)
    return call(
        factor_kernel,
        (
            jax.ShapeDtypeStruct((LEVELS, n, half), F32),
            jax.ShapeDtypeStruct((leaf, half), F32),
        ),
        grid_spec=pltpu.PrefetchScalarGridSpec(
            num_scalar_prefetch=1,
            grid=(1,),
            in_specs=[whole] * 6,
            out_specs=[pl.BlockSpec(memory_space=pl.ANY)] * 2,
            scratch_shapes=[
                pltpu.VMEM((2, *mine.shape), F32),
                pltpu.VMEM((count, LANES, LANES), F32),
                pltpu.VMEM((count, n, n), F32),
                pltpu.VMEM((count, n, n), F32),
                pltpu.VMEM((LEVELS, n, half), F32),
                pltpu.VMEM((steps, leaf // steps, half), F32),
                pltpu.SemaphoreType.DMA((steps + LEVELS,)),
            ],
        ),
    )(me, mine, theirs, *own, *other)


def beside(array, shift):
    count = lax.axis_size("leaf")
    pairs = [(i, i + shift) for i in range(count) if 0 <= i + shift < count]
    return lax.ppermute(array, "leaf", pairs)


def sibling(array, bit):
    return lax.ppermute(array, "leaf", [(i, i ^ 1 << bit) for i in range(lax.axis_size("leaf"))])


def other_core(array):
    return lax.ppermute(array, "probe", [(0, 1), (1, 0)])


def body(features, probes, lengthscale, near_blocks, leaf_order):
    blocks = near_blocks.shape[0]
    me = lax.axis_index("probe").astype(jnp.int32)[None]
    first = ((lax.axis_index("leaf") - 1) * blocks).astype(jnp.int32)[None]
    probes_before = beside(probes, 1)
    probes_after = beside(probes, -1)
    ordered = order_features(features, leaf_order)
    before = beside(ordered, 1)
    after = beside(ordered, -1)
    part, rows_t, far = near_part(near_blocks, first, lengthscale, ordered, probes)
    own = far_part(
        far, lengthscale, part, rows_t, before, after, probes_before, probes_after, blocks
    )
    other = other_core(own)
    block, *own_pieces = own_gram(own)
    gram, *other_pieces = gram_blocks(me, block, *own_pieces, other)
    grams = [gram]
    for depth in range(LEVELS):
        gram = gram + sibling(gram, depth)
        grams.append(gram)
    mine = jnp.concatenate(grams, 0)
    return factors(me, mine, other_core(mine), own_pieces, other_pieces)


def solution(mesh):
    in_specs = (P(None, "leaf"), P("probe", "leaf"), P(), P("leaf", None), P("leaf", None))
    out_specs = (P(None, "leaf", "probe"), P("leaf", "probe"))
    return jax.shard_map(body, mesh=mesh, in_specs=in_specs, out_specs=out_specs, check_vma=False)
```

```python
import math

import jax
import jax.numpy as jnp
from jax import lax
from jax.experimental import pallas as pl
from jax.experimental.pallas import tpu as pltpu
from jax.sharding import PartitionSpec as P

LEVELS = 4
LANES = 128
ROWS = 8
TILE = (ROWS, LANES)
LOG2_E = 1.4426950408889634
LN_2 = 0.6931471805599453
NUGGET = 2.0
TINY = 1e-20
HI = lax.Precision.HIGHEST
F32 = jnp.float32
BF16 = jnp.bfloat16
VMEM_BYTES = 14 << 20


def call(kernel, out_shape, **kwargs):
    return pl.pallas_call(
        kernel,
        out_shape=out_shape,
        compiler_params=pltpu.CompilerParams(vmem_limit_bytes=VMEM_BYTES),
        **kwargs,
    )


def dot(a, b, ca, cb, precision=HI):
    return lax.dot_general(
        a, b, (((ca,), (cb,)), ((), ())), precision=precision, preferred_element_type=F32
    )


def dot16(a, b, ca, cb):
    return lax.dot_general(a, b, (((ca,), (cb,)), ((), ())), preferred_element_type=F32)


def halves(x):
    hi = x.astype(BF16)
    return hi, (x - hi.astype(F32)).astype(BF16)


def thirds(x):
    hi = x.astype(BF16).astype(F32)
    rest = x - hi
    mid = rest.astype(BF16).astype(F32)
    return hi, mid, rest - mid


def in_hbm(array):
    return pltpu.with_memory_space_constraint(array, pltpu.HBM)


def order_kernel(feat_in, order_in, out, feat, order, sems):
    copies = [
        pltpu.make_async_copy(feat_in, feat, sems.at[0]),
        pltpu.make_async_copy(order_in, order, sems.at[1]),
    ]
    for copy in copies:
        copy.start()
    for copy in copies:
        copy.wait()
    chunks = feat.shape[1] // LANES
    pieces = [feat[:, c * LANES : (c + 1) * LANES].astype(F32) for c in range(chunks)]

    def one(q, carry):
        at = pl.multiple_of(q * LANES, LANES)
        index = jnp.broadcast_to(order[:, pl.ds(at, LANES)], TILE)
        low, high = index & (LANES - 1), index >> 7
        total = jnp.zeros(TILE, F32)
        for c in range(chunks):
            total = jnp.where(high == c, jnp.take_along_axis(pieces[c], low, axis=1), total)
        out[:, pl.ds(at, LANES)] = total.astype(BF16)
        return carry

    lax.fori_loop(0, chunks, one, 0)


def order_features(features, leaf_order):
    anywhere = pl.BlockSpec(memory_space=pltpu.HBM)
    return call(
        order_kernel,
        jax.ShapeDtypeStruct(features.shape, BF16),
        in_specs=[anywhere] * 2,
        out_specs=pl.BlockSpec(memory_space=pltpu.VMEM),
        scratch_shapes=[
            pltpu.VMEM(features.shape, BF16),
            pltpu.VMEM(leaf_order.shape, jnp.int32),
            pltpu.SemaphoreType.DMA((2,)),
        ],
    )(in_hbm(features), in_hbm(leaf_order))


SHIFT = 6
SLOTS = 160
WIDE = 4


def column_pieces(x, weight):
    norm = jnp.sum(x * x * weight, 0, keepdims=True)
    ones = jnp.ones_like(norm)
    zeros = jnp.zeros((2, x.shape[1]), F32)
    return jnp.concatenate([x, x, x, *thirds(norm), ones, ones, ones, zeros], 0).astype(BF16)


def row_pieces(x, weight):
    norm = jnp.sum(x * x * weight, 0, keepdims=True)
    ones = jnp.ones_like(norm)
    zeros = jnp.zeros((2, x.shape[1]), F32)
    return jnp.concatenate(
        [*thirds(-2.0 * weight * x), ones, ones, ones, *thirds(norm), zeros], 0
    ).T.astype(BF16)


def weights(scale):
    count = scale.shape[0]
    row = lax.broadcasted_iota(jnp.int32, (count, LANES), 0)
    held = jnp.full((count, LANES), scale[0], F32)
    for f in range(1, count):
        held = jnp.where(row == f, scale[f], held)
    return (3.0 * LOG2_E * LOG2_E) / (held * held)


def load_columns(cols, panel, feats, weight, blocks):
    block = feats[0].shape[1] // blocks
    for n, feat in enumerate(feats):
        pieces = column_pieces(feat[...].astype(F32), weight)
        for b in range(blocks):
            cols[n * blocks + b] = pieces[:, b * block : (b + 1) * block]
    last = len(feats) * blocks
    cols[last] = jnp.zeros(cols.shape[1:], BF16)
    panel[last] = jnp.zeros(panel.shape[1:], BF16)


def run_tasks(tasks, count, slot_of, rows_t, cols, panel, out, kerns):
    block = cols.shape[2]

    def where_of(n):
        code = tasks[n]
        at = pl.ds(pl.multiple_of((code >> SHIFT) * block, block), block)
        return at, slot_of(code & ((1 << SHIFT) - 1))

    def product(n, kern):
        at, slot = where_of(n)
        return at, dot16(kern, panel[slot], 1, 1)

    def some(i, carry):
        for half in range(2):
            group = 2 * i + half
            last = jnp.maximum(group - 1, 0)
            for u in range(WIDE):
                to, part = product(last * WIDE + u, kerns[1 - half][u])
                at, slot = where_of(group * WIDE + u)
                dist = jnp.maximum(dot16(rows_t[at, :], cols[slot], 1, 0), TINY)
                root = dist * lax.rsqrt(dist)
                kerns[half][u] = ((1.0 + LN_2 * root) * jnp.exp2(-root)).astype(BF16)
                out[to, :] += part
        return carry

    kerns[1][...] = jnp.zeros_like(kerns[1])
    pairs = (count + (2 * WIDE - 1)) // (2 * WIDE)
    lax.fori_loop(0, pairs, some, 0)
    for u in range(WIDE):
        to, part = product(jnp.maximum(2 * pairs - 1, 0) * WIDE + u, kerns[1][u])
        out[to, :] += part


def near_kernel(
    first, listed_in, scale_in, feat, probes, out, rows_t, far, weight_out,
    near_blocks, scale, tasks, cols, panel, k0, k1, sems,
):
    blocks, near = near_blocks.shape
    block = feat.shape[1] // blocks
    copies = [
        pltpu.make_async_copy(listed_in, near_blocks, sems.at[0]),
        pltpu.make_async_copy(scale_in, scale, sems.at[1]),
    ]
    for b in range(blocks):
        source = probes.at[:, b * block : (b + 1) * block]
        copies.append(pltpu.make_async_copy(source, panel.at[b], sems.at[2 + b]))
    for copy in copies:
        copy.start()
    copies[0].wait()

    def scan(a, counts):
        mine, rest = counts
        for j in range(near):
            listed = near_blocks[a, j] - first[0]
            code = (a << SHIFT) + listed
            inside = jnp.where((listed >= blocks) & (listed < 2 * blocks), 1, 0)
            tasks[mine] = code
            far[rest] = code
            mine = mine + inside
            rest = rest + (1 - inside)
        return mine, rest

    mine, rest = lax.fori_loop(0, blocks, scan, (jnp.int32(0), jnp.int32(0)))
    for u in range(2 * WIDE):
        tasks[mine + u] = 2 * blocks
        far[rest + u] = 3 * blocks
    far[SLOTS - 1] = rest

    copies[1].wait()
    weight_out[...] = weights(scale)
    weight = weight_out[:, :1]
    rows_t[...] = row_pieces(feat[...].astype(F32), weight)
    load_columns(cols, panel, [feat], weight, blocks)
    for copy in copies[2:]:
        copy.wait()
    here = lax.broadcasted_iota(jnp.int32, (block, block), 0)
    there = lax.broadcasted_iota(jnp.int32, (block, block), 1)
    nugget = jnp.where(here == there, NUGGET, 0.0).astype(BF16)
    for b in range(blocks):
        out[b * block : (b + 1) * block, :] = dot16(nugget, panel[b], 1, 1)
    run_tasks(tasks, mine, lambda listed: listed - blocks, rows_t, cols, panel, out, (k0, k1))


def near_part(near_blocks, first, scale, feat, probes):
    half, leaf = probes.shape
    blocks = near_blocks.shape[0]
    block = leaf // blocks
    whole = pl.BlockSpec(memory_space=pltpu.VMEM)
    anywhere = pl.BlockSpec(memory_space=pltpu.HBM)
    return call(
        near_kernel,
        (
            pltpu.VMEM((leaf, half), F32),
            pltpu.VMEM((leaf, 32), BF16),
            jax.ShapeDtypeStruct((SLOTS,), jnp.int32),
            pltpu.VMEM((ROWS, LANES), F32),
        ),
        grid_spec=pltpu.PrefetchScalarGridSpec(
            num_scalar_prefetch=1,
            grid=(1,),
            in_specs=[anywhere, anywhere, whole, anywhere],
            out_specs=[whole, whole, pl.BlockSpec(memory_space=pltpu.SMEM), whole],
            scratch_shapes=[
                pltpu.SMEM(near_blocks.shape, jnp.int32),
                pltpu.SMEM(scale.shape, F32),
                pltpu.SMEM((SLOTS,), jnp.int32),
                pltpu.VMEM((blocks + 1, 32, block), BF16),
                pltpu.VMEM((blocks + 1, half, block), BF16),
                *[pltpu.VMEM((WIDE, block, block), BF16)] * 2,
                pltpu.SemaphoreType.DMA((2 + blocks,)),
            ],
        ),
    )(first, in_hbm(near_blocks), in_hbm(scale), feat, in_hbm(probes))


def far_kernel(far, weight, part, rows_t, left, right, before, after, out, cols, panel, k0, k1):
    blocks = (cols.shape[0] - 1) // 2
    load_columns(cols, panel, [left, right], weight[:, :1], blocks)
    block = cols.shape[2]
    for n, probe in enumerate((before, after)):
        for b in range(blocks):
            panel[n * blocks + b] = probe[:, b * block : (b + 1) * block]
    out[...] = part[...]
    run_tasks(
        far,
        far[SLOTS - 1],
        lambda listed: jnp.where(listed < blocks, listed, listed - blocks),
        rows_t,
        cols,
        panel,
        out,
        (k0, k1),
    )


def far_part(far, weight, part, rows_t, left, right, before, after, blocks):
    half, leaf = before.shape
    block = leaf // blocks
    whole = pl.BlockSpec(memory_space=pltpu.VMEM)
    return call(
        far_kernel,
        pltpu.VMEM((leaf, half), F32),
        grid_spec=pltpu.PrefetchScalarGridSpec(
            num_scalar_prefetch=1,
            grid=(1,),
            in_specs=[whole] * 7,
            out_specs=whole,
            scratch_shapes=[
                pltpu.VMEM((2 * blocks + 1, 32, block), BF16),
                pltpu.VMEM((2 * blocks + 1, half, block), BF16),
                *[pltpu.VMEM((WIDE, block, block), BF16)] * 2,
            ],
        ),
    )(far, weight, part, rows_t, left, right, before, after)


HALF = LANES // 2
PACKED = HALF + ROWS


def pack(block):
    shape = (HALF, LANES)
    row = lax.broadcasted_iota(jnp.int32, shape, 0)
    col = lax.broadcasted_iota(jnp.int32, shape, 1) - HALF
    bottom = block[HALF:, :]
    top = pltpu.roll(block[:HALF, :], HALF, 1)
    diagonal = jnp.sum(jnp.where(row == col, bottom, 0.0), 0, keepdims=True)
    body = jnp.where((col >= 0) & (row >= col), top, bottom)
    return body, jnp.broadcast_to(diagonal, TILE)


def unpack(body, diagonal):
    shape = (HALF, HALF)
    row = lax.broadcasted_iota(jnp.int32, shape, 0)
    col = lax.broadcasted_iota(jnp.int32, shape, 1)
    side = body[:, :HALF]
    fold = body[:, HALF:]
    flip = fold.T
    top = jnp.where(row >= col, fold, flip)
    bottom = jnp.where(row < col, fold, flip)
    bottom = jnp.where(row == col, diagonal[:1, HALF:], bottom)
    return jnp.concatenate(
        [jnp.concatenate([top, side.T], 1), jnp.concatenate([side, bottom], 1)], 0
    )


def product(a, b):
    return dot16(a[0], b[0], 0, 0) + (dot16(a[0], b[1], 0, 0) + dot16(a[1], b[0], 0, 0))


def own_kernel(own, out, high, low):
    a0, a1 = halves(own[...])
    high[...] = a0
    low[...] = a1
    out[:HALF], out[HALF:] = pack(product((a0, a1), (a0, a1)))


def own_gram(own):
    leaf, half = own.shape
    return call(
        own_kernel,
        (
            pltpu.VMEM((PACKED, half), F32),
            pltpu.VMEM((leaf, half), BF16),
            pltpu.VMEM((leaf, half), BF16),
        ),
    )(own)


def gram_kernel(me, block, high, low, other, out, highs, lows):
    n = LANES
    b0, b1 = halves(other[...])
    highs[:, :n], highs[:, n:] = high[...], b0
    lows[:, :n], lows[:, n:] = low[...], b1
    out[:PACKED] = block[...]

    @pl.when(me[0] == 0)
    def _():
        out[PACKED:] = product((b0[:, :HALF], b1[:, :HALF]), (high[...], low[...]))

    @pl.when(me[0] == 1)
    def _():
        out[PACKED:] = product((high[:, HALF:], low[:, HALF:]), (b0, b1))


def gram_blocks(me, block, high, low, other):
    leaf, half = other.shape
    whole = pl.BlockSpec(memory_space=pltpu.VMEM)
    return call(
        gram_kernel,
        (
            jax.ShapeDtypeStruct((PACKED + HALF, half), F32),
            pltpu.VMEM((leaf, 2 * half), BF16),
            pltpu.VMEM((leaf, 2 * half), BF16),
        ),
        grid_spec=pltpu.PrefetchScalarGridSpec(
            num_scalar_prefetch=1, grid=(1,), in_specs=[whole] * 4, out_specs=[whole] * 3
        ),
    )(me, block, high, low, other)


def row_of(x, k):
    return jnp.broadcast_to(x[k : k + 1, :], TILE)


def columns(panel, at):
    return [
        jnp.take_along_axis(panel, jnp.full(TILE, at + m, jnp.int32), axis=1)
        for m in range(ROWS)
    ]


def outer_pieces(a, b):
    a0, a1, a2 = thirds(a)
    b0, b1, b2 = thirds(b)
    left = jnp.concatenate([a0, a0, a1, a0, a1, a2], 0).astype(BF16)
    right = jnp.concatenate([b0, b1, b0, b2, b1, b0], 0).astype(BF16)
    return left, right


def eliminate(panels, nexts, at):
    count = range(len(panels))
    lane = lax.broadcasted_iota(jnp.int32, TILE, 1)
    sub = lax.broadcasted_iota(jnp.int32, TILE, 0)
    here = (lane >= at) & (lane < at + ROWS)
    unit = jnp.where(lane - at == sub, 1.0, 0.0)
    cols = [columns(panels[l], at) for l in count]
    rows = [jnp.where(here, unit, panels[l]) for l in count]
    lows = [jnp.zeros(TILE, F32) for l in count]
    below = [columns(panel, at) for panel in nexts]
    nexts = [jnp.where(here, 0.0, panel) for panel in nexts]
    for k in range(ROWS):
        inv = [lax.rsqrt(row_of(cols[l][k], k)) for l in count]
        low = [jnp.where(sub >= k, cols[l][k] * inv[l], 0.0) for l in count]
        for l in count:
            lead = row_of(rows[l], k) * inv[l]
            rows[l] = jnp.where(sub == k, lead, rows[l] - low[l] * lead)
            lows[l] = jnp.where(lane == at + k, low[l], lows[l])
            if nexts:
                below[l][k] = below[l][k] * inv[l]
                nexts[l] = nexts[l] - below[l][k] * lead
        for m in range(k + 1, ROWS):
            for l in count:
                one = row_of(low[l], m)
                cols[l][m] = cols[l][m] - low[l] * one
                if nexts:
                    below[l][m] = below[l][m] - below[l][k] * one
    return rows, lows, nexts


def factor_block(work, ups, invs, base):
    count = range(work.shape[0])
    lane = lax.broadcasted_iota(jnp.int32, TILE, 1)
    span = slice(base, base + LANES)
    pair = 2 * ROWS
    for at in range(0, LANES, pair):
        mid, end = at + ROWS, at + pair
        both = [work[l, at:end, :] for l in count]
        first, low_first, second = eliminate(
            [b[:ROWS] for b in both], [b[ROWS:] for b in both], at
        )
        second, low_second, _ = eliminate(second, [], mid)
        for l in count:
            for x, low, p in ((first, low_first, at), (second, low_second, mid)):
                to = slice(base + p, base + p + ROWS)
                ups[l, to, span] = jnp.where(lane >= p + ROWS, x[l], low[l])
                invs[l, to, span] = jnp.where(lane < p + ROWS, x[l], 0.0)
        if end == LANES:
            break
        lefts, rights = [], []
        for l in count:
            lefts.append(jnp.concatenate([first[l], second[l]], 0))
            rights.append(
                jnp.concatenate(
                    [jnp.where((lane >= mid) & (lane < end), 0.0, first[l]), second[l]], 0
                )
            )
        pieces = [outer_pieces(lefts[l], rights[l]) for l in count]
        col = lax.broadcasted_iota(jnp.int32, (LANES - end, LANES), 1)
        gone = (col >= at) & (col < end)
        sums = [dot16(pieces[l][0][:, end:], pieces[l][1], 0, 0) for l in count]
        for l in count:
            work[l, end:, :] = jnp.where(gone, 0.0, work[l, end:, :]) - sums[l]


def straighten(ups, l, base):
    n = LANES
    block = ups[l, base : base + n, base : base + n]
    row = lax.broadcasted_iota(jnp.int32, (n, n), 0)
    col = lax.broadcasted_iota(jnp.int32, (n, n), 1)
    ups[l, base : base + n, base : base + n] = jnp.where(row >> 3 == col >> 3, block.T, block)


def factor(grams, work, ups, invs):
    n = LANES
    blank = jnp.zeros((n, n), F32)
    count = range(work.shape[0])
    for l in count:
        work[l] = grams(l, 0)
    factor_block(work, ups, invs, 0)
    sides = [dot(invs[l, 0:n, 0:n], grams(l, 1), 1, 1) for l in count]
    for l in count:
        ups[l, 0:n, n : 2 * n] = sides[l]
        ups[l, n : 2 * n, 0:n] = blank
        invs[l, 0:n, n : 2 * n] = blank
    squares = [dot(sides[l], sides[l], 0, 0) for l in count]
    for l in count:
        work[l] = grams(l, 2) - squares[l]
    factor_block(work, ups, invs, n)
    downs = [dot(ups[l, 0:n, n : 2 * n], invs[l, 0:n, 0:n], 0, 0) for l in count]
    downs = [dot(invs[l, n : 2 * n, n : 2 * n], downs[l], 1, 0) for l in count]
    for l in count:
        invs[l, n : 2 * n, 0:n] = -downs[l]
        straighten(ups, l, 0)
        straighten(ups, l, n)


def factor_kernel(
    me, mine, theirs, highs, lows, transfer, basis, pieces, work, ups, invs, moved, rows, sems
):
    n = LANES
    height = PACKED + HALF
    pieces[me[0]] = mine[...]
    pieces[1 - me[0]] = theirs[...]

    def gram(l, b):
        at = l * height
        if b == 1:
            return jnp.concatenate([pieces[p, at + PACKED : at + height, :] for p in range(2)], 0)
        part = pieces.at[b // 2]
        return unpack(part[at : at + HALF, :], part[at + HALF : at + PACKED, :])

    factor(gram, work, ups, invs)
    cols = pl.ds(pl.multiple_of(me[0] * n, n), n)
    rest = pl.ds(pl.multiple_of((1 - me[0]) * n, n), n)
    scale = math.sqrt(2**LEVELS * highs.shape[0])
    weight = invs.at[LEVELS]
    high, low = halves(jnp.concatenate([weight[cols, cols], weight[cols, rest]], 1) * scale)
    both = jnp.concatenate([high, low], 0)
    steps, size, _ = rows.shape
    copies = []
    for s in range(steps):
        at = slice(s * size, (s + 1) * size)
        two = dot16(highs[at, :], both, 1, 1)
        rows[s] = two[:, :n] + (two[:, n:] + dot16(lows[at, :], high, 1, 1))
        copies.append(pltpu.make_async_copy(rows.at[s], basis.at[pl.ds(s * size, size)], sems.at[s]))
        copies[-1].start()
    for l in range(LEVELS):
        moved[l] = dot(ups[l], invs[l + 1, cols, :], 1, 1)
        copies.append(pltpu.make_async_copy(moved.at[l], transfer.at[l], sems.at[steps + l]))
        copies[-1].start()
    for copy in copies:
        copy.wait()


def factors(me, mine, theirs, highs, lows):
    n = 2 * LANES
    count = LEVELS + 1
    leaf, half = highs.shape[0], LANES
    steps = 6
    whole = pl.BlockSpec(memory_space=pltpu.VMEM)
    return call(
        factor_kernel,
        (
            jax.ShapeDtypeStruct((LEVELS, n, half), F32),
            jax.ShapeDtypeStruct((leaf, half), F32),
        ),
        grid_spec=pltpu.PrefetchScalarGridSpec(
            num_scalar_prefetch=1,
            grid=(1,),
            in_specs=[whole] * 4,
            out_specs=[pl.BlockSpec(memory_space=pl.ANY)] * 2,
            scratch_shapes=[
                pltpu.VMEM((2, *mine.shape), F32),
                pltpu.VMEM((count, LANES, LANES), F32),
                pltpu.VMEM((count, n, n), F32),
                pltpu.VMEM((count, n, n), F32),
                pltpu.VMEM((LEVELS, n, half), F32),
                pltpu.VMEM((steps, leaf // steps, half), F32),
                pltpu.SemaphoreType.DMA((steps + LEVELS,)),
            ],
        ),
    )(me, mine, theirs, highs, lows)


def beside(array, shift):
    count = lax.axis_size("leaf")
    pairs = [(i, i + shift) for i in range(count) if 0 <= i + shift < count]
    return lax.ppermute(array, "leaf", pairs)


def sibling(array, bit):
    return lax.ppermute(array, "leaf", [(i, i ^ 1 << bit) for i in range(lax.axis_size("leaf"))])


def other_core(array):
    return lax.ppermute(array, "probe", [(0, 1), (1, 0)])


def body(features, probes, lengthscale, near_blocks, leaf_order):
    blocks = near_blocks.shape[0]
    me = lax.axis_index("probe").astype(jnp.int32)[None]
    first = ((lax.axis_index("leaf") - 1) * blocks).astype(jnp.int32)[None]
    probes_before = beside(probes, 1)
    probes_after = beside(probes, -1)
    ordered = order_features(features, leaf_order)
    before = beside(ordered, 1)
    after = beside(ordered, -1)
    part, rows_t, far, weight = near_part(near_blocks, first, lengthscale, ordered, probes)
    own = far_part(
        far, weight, part, rows_t, before, after, probes_before, probes_after, blocks
    )
    other = other_core(own)
    block, high, low = own_gram(own)
    gram, highs, lows = gram_blocks(me, block, high, low, other)
    grams = [gram]
    for depth in range(LEVELS):
        gram = gram + sibling(gram, depth)
        grams.append(gram)
    mine = jnp.concatenate(grams, 0)
    return factors(me, mine, other_core(mine), highs, lows)


def solution(mesh):
    in_specs = (P(None, "leaf"), P("probe", "leaf"), P(), P("leaf", None), P("leaf", None))
    out_specs = (P(None, "leaf", "probe"), P("leaf", "probe"))
    return jax.shard_map(body, mesh=mesh, in_specs=in_specs, out_specs=out_specs, check_vma=False)
```

```python
import math

import jax
import jax.numpy as jnp
from jax import lax
from jax.experimental import pallas as pl
from jax.experimental.pallas import tpu as pltpu
from jax.sharding import PartitionSpec as P

LEVELS = 4
LANES = 128
ROWS = 8
TILE = (ROWS, LANES)
LOG2_E = 1.4426950408889634
LN_2 = 0.6931471805599453
NUGGET = 2.0
TINY = 1e-20
HI = lax.Precision.HIGHEST
F32 = jnp.float32
BF16 = jnp.bfloat16
VMEM_BYTES = 14 << 20


def call(kernel, out_shape, **kwargs):
    return pl.pallas_call(
        kernel,
        out_shape=out_shape,
        compiler_params=pltpu.CompilerParams(vmem_limit_bytes=VMEM_BYTES),
        **kwargs,
    )


def dot(a, b, ca, cb, precision=HI):
    return lax.dot_general(
        a, b, (((ca,), (cb,)), ((), ())), precision=precision, preferred_element_type=F32
    )


def dot16(a, b, ca, cb):
    return lax.dot_general(a, b, (((ca,), (cb,)), ((), ())), preferred_element_type=F32)


def halves(x):
    hi = x.astype(BF16)
    return hi, (x - hi.astype(F32)).astype(BF16)


def thirds(x):
    hi = x.astype(BF16).astype(F32)
    rest = x - hi
    mid = rest.astype(BF16).astype(F32)
    return hi, mid, rest - mid


def in_hbm(array):
    return pltpu.with_memory_space_constraint(array, pltpu.HBM)


def order_kernel(feat_in, order_in, out, feat, order, sems):
    copies = [
        pltpu.make_async_copy(feat_in, feat, sems.at[0]),
        pltpu.make_async_copy(order_in, order, sems.at[1]),
    ]
    for copy in copies:
        copy.start()
    for copy in copies:
        copy.wait()
    chunks = feat.shape[1] // LANES
    pieces = [feat[:, c * LANES : (c + 1) * LANES].astype(F32) for c in range(chunks)]

    def one(q, carry):
        at = pl.multiple_of(q * LANES, LANES)
        index = jnp.broadcast_to(order[:, pl.ds(at, LANES)], TILE)
        low, high = index & (LANES - 1), index >> 7
        total = jnp.zeros(TILE, F32)
        for c in range(chunks):
            total = jnp.where(high == c, jnp.take_along_axis(pieces[c], low, axis=1), total)
        out[:, pl.ds(at, LANES)] = total.astype(BF16)
        return carry

    lax.fori_loop(0, chunks, one, 0)


def order_features(features, leaf_order):
    anywhere = pl.BlockSpec(memory_space=pltpu.HBM)
    return call(
        order_kernel,
        jax.ShapeDtypeStruct(features.shape, BF16),
        in_specs=[anywhere] * 2,
        out_specs=pl.BlockSpec(memory_space=pltpu.VMEM),
        scratch_shapes=[
            pltpu.VMEM(features.shape, BF16),
            pltpu.VMEM(leaf_order.shape, jnp.int32),
            pltpu.SemaphoreType.DMA((2,)),
        ],
    )(in_hbm(features), in_hbm(leaf_order))


SHIFT = 6
SLOTS = 160
WIDE = 4


def column_pieces(x, weight):
    norm = jnp.sum(x * x * weight, 0, keepdims=True)
    ones = jnp.ones_like(norm)
    zeros = jnp.zeros((2, x.shape[1]), F32)
    return jnp.concatenate([x, x, x, *thirds(norm), ones, ones, ones, zeros], 0).astype(BF16)


def row_pieces(x, weight):
    norm = jnp.sum(x * x * weight, 0, keepdims=True)
    ones = jnp.ones_like(norm)
    zeros = jnp.zeros((2, x.shape[1]), F32)
    return jnp.concatenate(
        [*thirds(-2.0 * weight * x), ones, ones, ones, *thirds(norm), zeros], 0
    ).T.astype(BF16)


def weights(scale):
    count = scale.shape[0]
    row = lax.broadcasted_iota(jnp.int32, (count, LANES), 0)
    held = jnp.full((count, LANES), scale[0], F32)
    for f in range(1, count):
        held = jnp.where(row == f, scale[f], held)
    return (3.0 * LOG2_E * LOG2_E) / (held * held)


def load_columns(cols, panel, feats, weight, blocks):
    block = feats[0].shape[1] // blocks
    for n, feat in enumerate(feats):
        pieces = column_pieces(feat[...].astype(F32), weight)
        for b in range(blocks):
            cols[n * blocks + b] = pieces[:, b * block : (b + 1) * block]
    last = len(feats) * blocks
    cols[last] = jnp.zeros(cols.shape[1:], BF16)
    panel[last] = jnp.zeros(panel.shape[1:], BF16)


def run_tasks(tasks, count, slot_of, rows_t, cols, panel, out, kerns):
    block = cols.shape[2]

    def where_of(n):
        code = tasks[n]
        at = pl.ds(pl.multiple_of((code >> SHIFT) * block, block), block)
        return at, slot_of(code & ((1 << SHIFT) - 1))

    def product(n, kern):
        at, slot = where_of(n)
        return at, dot16(kern, panel[slot], 1, 1)

    def some(i, carry):
        for half in range(2):
            group = 2 * i + half
            last = jnp.maximum(group - 1, 0)
            for u in range(WIDE):
                to, part = product(last * WIDE + u, kerns[1 - half][u])
                at, slot = where_of(group * WIDE + u)
                dist = jnp.maximum(dot16(rows_t[at, :], cols[slot], 1, 0), TINY)
                root = dist * lax.rsqrt(dist)
                kerns[half][u] = ((1.0 + LN_2 * root) * jnp.exp2(-root)).astype(BF16)
                out[to, :] += part
        return carry

    kerns[1][...] = jnp.zeros_like(kerns[1])
    pairs = (count + (2 * WIDE - 1)) // (2 * WIDE)
    lax.fori_loop(0, pairs, some, 0)
    for u in range(WIDE):
        to, part = product(jnp.maximum(2 * pairs - 1, 0) * WIDE + u, kerns[1][u])
        out[to, :] += part


def near_kernel(
    first, listed_in, scale_in, feat, probes, out, rows_t, far, weight_out,
    near_blocks, scale, tasks, cols, panel, k0, k1, sems,
):
    blocks, near = near_blocks.shape
    block = feat.shape[1] // blocks
    copies = [
        pltpu.make_async_copy(listed_in, near_blocks, sems.at[0]),
        pltpu.make_async_copy(scale_in, scale, sems.at[1]),
    ]
    for b in range(blocks):
        source = probes.at[:, b * block : (b + 1) * block]
        copies.append(pltpu.make_async_copy(source, panel.at[b], sems.at[2 + b]))
    for copy in copies:
        copy.start()
    copies[0].wait()

    def scan(a, counts):
        mine, rest = counts
        for j in range(near):
            listed = near_blocks[a, j] - first[0]
            code = (a << SHIFT) + listed
            inside = jnp.where((listed >= blocks) & (listed < 2 * blocks), 1, 0)
            tasks[mine] = code
            far[rest] = code
            mine = mine + inside
            rest = rest + (1 - inside)
        return mine, rest

    mine, rest = lax.fori_loop(0, blocks, scan, (jnp.int32(0), jnp.int32(0)))
    for u in range(2 * WIDE):
        tasks[mine + u] = 2 * blocks
        far[rest + u] = 3 * blocks
    far[SLOTS - 1] = rest

    copies[1].wait()
    weight_out[...] = weights(scale)
    weight = weight_out[:, :1]
    rows_t[...] = row_pieces(feat[...].astype(F32), weight)
    load_columns(cols, panel, [feat], weight, blocks)
    for copy in copies[2:]:
        copy.wait()
    here = lax.broadcasted_iota(jnp.int32, (block, block), 0)
    there = lax.broadcasted_iota(jnp.int32, (block, block), 1)
    nugget = jnp.where(here == there, NUGGET, 0.0).astype(BF16)
    for b in range(blocks):
        out[b * block : (b + 1) * block, :] = dot16(nugget, panel[b], 1, 1)
    run_tasks(tasks, mine, lambda listed: listed - blocks, rows_t, cols, panel, out, (k0, k1))


def near_part(near_blocks, first, scale, feat, probes):
    half, leaf = probes.shape
    blocks = near_blocks.shape[0]
    block = leaf // blocks
    whole = pl.BlockSpec(memory_space=pltpu.VMEM)
    anywhere = pl.BlockSpec(memory_space=pltpu.HBM)
    return call(
        near_kernel,
        (
            pltpu.VMEM((leaf, half), F32),
            pltpu.VMEM((leaf, 32), BF16),
            jax.ShapeDtypeStruct((SLOTS,), jnp.int32),
            pltpu.VMEM((ROWS, LANES), F32),
        ),
        grid_spec=pltpu.PrefetchScalarGridSpec(
            num_scalar_prefetch=1,
            grid=(1,),
            in_specs=[anywhere, anywhere, whole, anywhere],
            out_specs=[whole, whole, pl.BlockSpec(memory_space=pltpu.SMEM), whole],
            scratch_shapes=[
                pltpu.SMEM(near_blocks.shape, jnp.int32),
                pltpu.SMEM(scale.shape, F32),
                pltpu.SMEM((SLOTS,), jnp.int32),
                pltpu.VMEM((blocks + 1, 32, block), BF16),
                pltpu.VMEM((blocks + 1, half, block), BF16),
                *[pltpu.VMEM((WIDE, block, block), BF16)] * 2,
                pltpu.SemaphoreType.DMA((2 + blocks,)),
            ],
        ),
    )(first, in_hbm(near_blocks), in_hbm(scale), feat, in_hbm(probes))


def far_kernel(far, weight, part, rows_t, left, right, before, after, out, cols, panel, k0, k1):
    blocks = (cols.shape[0] - 1) // 2
    load_columns(cols, panel, [left, right], weight[:, :1], blocks)
    block = cols.shape[2]
    for n, probe in enumerate((before, after)):
        for b in range(blocks):
            panel[n * blocks + b] = probe[:, b * block : (b + 1) * block]
    out[...] = part[...]
    run_tasks(
        far,
        far[SLOTS - 1],
        lambda listed: jnp.where(listed < blocks, listed, listed - blocks),
        rows_t,
        cols,
        panel,
        out,
        (k0, k1),
    )


def far_part(far, weight, part, rows_t, left, right, before, after, blocks):
    half, leaf = before.shape
    block = leaf // blocks
    whole = pl.BlockSpec(memory_space=pltpu.VMEM)
    return call(
        far_kernel,
        pltpu.VMEM((leaf, half), F32),
        grid_spec=pltpu.PrefetchScalarGridSpec(
            num_scalar_prefetch=1,
            grid=(1,),
            in_specs=[whole] * 7,
            out_specs=whole,
            scratch_shapes=[
                pltpu.VMEM((2 * blocks + 1, 32, block), BF16),
                pltpu.VMEM((2 * blocks + 1, half, block), BF16),
                *[pltpu.VMEM((WIDE, block, block), BF16)] * 2,
            ],
        ),
    )(far, weight, part, rows_t, left, right, before, after)


HALF = LANES // 2
PACKED = HALF + ROWS


def pack(block):
    shape = (HALF, LANES)
    row = lax.broadcasted_iota(jnp.int32, shape, 0)
    col = lax.broadcasted_iota(jnp.int32, shape, 1) - HALF
    bottom = block[HALF:, :]
    top = pltpu.roll(block[:HALF, :], HALF, 1)
    diagonal = jnp.sum(jnp.where(row == col, bottom, 0.0), 0, keepdims=True)
    body = jnp.where((col >= 0) & (row >= col), top, bottom)
    return body, jnp.broadcast_to(diagonal, TILE)


def unpack(body, diagonal):
    shape = (HALF, HALF)
    row = lax.broadcasted_iota(jnp.int32, shape, 0)
    col = lax.broadcasted_iota(jnp.int32, shape, 1)
    side = body[:, :HALF]
    fold = body[:, HALF:]
    flip = fold.T
    top = jnp.where(row >= col, fold, flip)
    bottom = jnp.where(row < col, fold, flip)
    bottom = jnp.where(row == col, diagonal[:1, HALF:], bottom)
    return jnp.concatenate(
        [jnp.concatenate([top, side.T], 1), jnp.concatenate([side, bottom], 1)], 0
    )


def product(a, b):
    return dot16(a[0], b[0], 0, 0) + (dot16(a[0], b[1], 0, 0) + dot16(a[1], b[0], 0, 0))


def own_kernel(own, out, high, low):
    a0, a1 = halves(own[...])
    high[:, :LANES] = a0
    low[:, :LANES] = a1
    out[:HALF], out[HALF:] = pack(product((a0, a1), (a0, a1)))


def own_gram(own):
    leaf, half = own.shape
    return call(
        own_kernel,
        (
            pltpu.VMEM((PACKED, half), F32),
            pltpu.VMEM((leaf, 2 * half), BF16),
            pltpu.VMEM((leaf, 2 * half), BF16),
        ),
    )(own)


def gram_kernel(me, block, high, low, other, out, highs, lows):
    n = LANES
    b0, b1 = halves(other[...])
    a0, a1 = high.at[:, :n], low.at[:, :n]
    highs[:, n:] = b0
    lows[:, n:] = b1
    out[:PACKED] = block[...]

    @pl.when(me[0] == 0)
    def _():
        out[PACKED:] = product((b0[:, :HALF], b1[:, :HALF]), (a0[...], a1[...]))

    @pl.when(me[0] == 1)
    def _():
        out[PACKED:] = product((high[:, HALF:n], low[:, HALF:n]), (b0, b1))


def gram_blocks(me, block, high, low, other):
    leaf, half = other.shape
    whole = pl.BlockSpec(memory_space=pltpu.VMEM)
    return call(
        gram_kernel,
        (
            jax.ShapeDtypeStruct((PACKED + HALF, half), F32),
            pltpu.VMEM((leaf, 2 * half), BF16),
            pltpu.VMEM((leaf, 2 * half), BF16),
        ),
        grid_spec=pltpu.PrefetchScalarGridSpec(
            num_scalar_prefetch=1, grid=(1,), in_specs=[whole] * 4, out_specs=[whole] * 3
        ),
        input_output_aliases={2: 1, 3: 2},
    )(me, block, high, low, other)


def row_of(x, k):
    return jnp.broadcast_to(x[k : k + 1, :], TILE)


def columns(panel, at):
    return [
        jnp.take_along_axis(panel, jnp.full(TILE, at + m, jnp.int32), axis=1)
        for m in range(ROWS)
    ]


def outer_pieces(a, b):
    a0, a1, a2 = thirds(a)
    b0, b1, b2 = thirds(b)
    left = jnp.concatenate([a0, a0, a1, a0, a1, a2], 0).astype(BF16)
    right = jnp.concatenate([b0, b1, b0, b2, b1, b0], 0).astype(BF16)
    return left, right


def eliminate(panels, nexts, at):
    count = range(len(panels))
    lane = lax.broadcasted_iota(jnp.int32, TILE, 1)
    sub = lax.broadcasted_iota(jnp.int32, TILE, 0)
    here = (lane >= at) & (lane < at + ROWS)
    unit = jnp.where(lane - at == sub, 1.0, 0.0)
    cols = [columns(panels[l], at) for l in count]
    rows = [jnp.where(here, unit, panels[l]) for l in count]
    lows = [jnp.zeros(TILE, F32) for l in count]
    below = [columns(panel, at) for panel in nexts]
    nexts = [jnp.where(here, 0.0, panel) for panel in nexts]
    for k in range(ROWS):
        inv = [lax.rsqrt(row_of(cols[l][k], k)) for l in count]
        low = [jnp.where(sub >= k, cols[l][k] * inv[l], 0.0) for l in count]
        for l in count:
            lead = row_of(rows[l], k) * inv[l]
            rows[l] = jnp.where(sub == k, lead, rows[l] - low[l] * lead)
            lows[l] = jnp.where(lane == at + k, low[l], lows[l])
            if nexts:
                below[l][k] = below[l][k] * inv[l]
                nexts[l] = nexts[l] - below[l][k] * lead
        for m in range(k + 1, ROWS):
            for l in count:
                one = row_of(low[l], m)
                cols[l][m] = cols[l][m] - low[l] * one
                if nexts:
                    below[l][m] = below[l][m] - below[l][k] * one
    return rows, lows, nexts


def factor_block(work, ups, invs, base):
    count = range(work.shape[0])
    lane = lax.broadcasted_iota(jnp.int32, TILE, 1)
    span = slice(base, base + LANES)
    pair = 2 * ROWS
    for at in range(0, LANES, pair):
        mid, end = at + ROWS, at + pair
        both = [work[l, at:end, :] for l in count]
        first, low_first, second = eliminate(
            [b[:ROWS] for b in both], [b[ROWS:] for b in both], at
        )
        second, low_second, _ = eliminate(second, [], mid)
        for l in count:
            for x, low, p in ((first, low_first, at), (second, low_second, mid)):
                to = slice(base + p, base + p + ROWS)
                ups[l, to, span] = jnp.where(lane >= p + ROWS, x[l], low[l])
                invs[l, to, span] = jnp.where(lane < p + ROWS, x[l], 0.0)
        if end == LANES:
            break
        lefts, rights = [], []
        for l in count:
            lefts.append(jnp.concatenate([first[l], second[l]], 0))
            rights.append(
                jnp.concatenate(
                    [jnp.where((lane >= mid) & (lane < end), 0.0, first[l]), second[l]], 0
                )
            )
        pieces = [outer_pieces(lefts[l], rights[l]) for l in count]
        col = lax.broadcasted_iota(jnp.int32, (LANES - end, LANES), 1)
        gone = (col >= at) & (col < end)
        sums = [dot16(pieces[l][0][:, end:], pieces[l][1], 0, 0) for l in count]
        for l in count:
            work[l, end:, :] = jnp.where(gone, 0.0, work[l, end:, :]) - sums[l]


def straighten(ups, l, base):
    n = LANES
    block = ups[l, base : base + n, base : base + n]
    row = lax.broadcasted_iota(jnp.int32, (n, n), 0)
    col = lax.broadcasted_iota(jnp.int32, (n, n), 1)
    ups[l, base : base + n, base : base + n] = jnp.where(row >> 3 == col >> 3, block.T, block)


def factor(grams, work, ups, invs):
    n = LANES
    blank = jnp.zeros((n, n), F32)
    count = range(work.shape[0])
    for l in count:
        work[l] = grams(l, 0)
    factor_block(work, ups, invs, 0)
    sides = [dot(invs[l, 0:n, 0:n], grams(l, 1), 1, 1) for l in count]
    for l in count:
        ups[l, 0:n, n : 2 * n] = sides[l]
        ups[l, n : 2 * n, 0:n] = blank
        invs[l, 0:n, n : 2 * n] = blank
    squares = [dot(sides[l], sides[l], 0, 0) for l in count]
    for l in count:
        work[l] = grams(l, 2) - squares[l]
    factor_block(work, ups, invs, n)
    downs = [dot(ups[l, 0:n, n : 2 * n], invs[l, 0:n, 0:n], 0, 0) for l in count]
    downs = [dot(invs[l, n : 2 * n, n : 2 * n], downs[l], 1, 0) for l in count]
    for l in count:
        invs[l, n : 2 * n, 0:n] = -downs[l]
        straighten(ups, l, 0)
        straighten(ups, l, n)


def factor_kernel(
    me, mine, theirs, highs, lows, transfer, basis, pieces, work, ups, invs, moved, rows, sems
):
    n = LANES
    height = PACKED + HALF
    pieces[me[0]] = mine[...]
    pieces[1 - me[0]] = theirs[...]

    def gram(l, b):
        at = l * height
        if b == 1:
            return jnp.concatenate([pieces[p, at + PACKED : at + height, :] for p in range(2)], 0)
        part = pieces.at[b // 2]
        return unpack(part[at : at + HALF, :], part[at + HALF : at + PACKED, :])

    factor(gram, work, ups, invs)
    cols = pl.ds(pl.multiple_of(me[0] * n, n), n)
    rest = pl.ds(pl.multiple_of((1 - me[0]) * n, n), n)
    scale = math.sqrt(2**LEVELS * highs.shape[0])
    weight = invs.at[LEVELS]
    high, low = halves(jnp.concatenate([weight[cols, cols], weight[cols, rest]], 1) * scale)
    both = jnp.concatenate([high, low], 0)
    steps, size, _ = rows.shape
    copies = []
    for s in range(steps):
        at = slice(s * size, (s + 1) * size)
        two = dot16(highs[at, :], both, 1, 1)
        rows[s] = two[:, :n] + (two[:, n:] + dot16(lows[at, :], high, 1, 1))
        copies.append(pltpu.make_async_copy(rows.at[s], basis.at[pl.ds(s * size, size)], sems.at[s]))
        copies[-1].start()
    for l in range(LEVELS):
        moved[l] = dot(ups[l], invs[l + 1, cols, :], 1, 1)
        copies.append(pltpu.make_async_copy(moved.at[l], transfer.at[l], sems.at[steps + l]))
        copies[-1].start()
    for copy in copies:
        copy.wait()


def factors(me, mine, theirs, highs, lows):
    n = 2 * LANES
    count = LEVELS + 1
    leaf, half = highs.shape[0], LANES
    steps = 6
    whole = pl.BlockSpec(memory_space=pltpu.VMEM)
    return call(
        factor_kernel,
        (
            jax.ShapeDtypeStruct((LEVELS, n, half), F32),
            jax.ShapeDtypeStruct((leaf, half), F32),
        ),
        grid_spec=pltpu.PrefetchScalarGridSpec(
            num_scalar_prefetch=1,
            grid=(1,),
            in_specs=[whole] * 4,
            out_specs=[pl.BlockSpec(memory_space=pl.ANY)] * 2,
            scratch_shapes=[
                pltpu.VMEM((2, *mine.shape), F32),
                pltpu.VMEM((count, LANES, LANES), F32),
                pltpu.VMEM((count, n, n), F32),
                pltpu.VMEM((count, n, n), F32),
                pltpu.VMEM((LEVELS, n, half), F32),
                pltpu.VMEM((steps, leaf // steps, half), F32),
                pltpu.SemaphoreType.DMA((steps + LEVELS,)),
            ],
        ),
    )(me, mine, theirs, highs, lows)


def beside(array, shift):
    count = lax.axis_size("leaf")
    pairs = [(i, i + shift) for i in range(count) if 0 <= i + shift < count]
    return lax.ppermute(array, "leaf", pairs)


def sibling(array, flip):
    return lax.ppermute(array, "leaf", [(i, i ^ flip) for i in range(lax.axis_size("leaf"))])


def other_core(array):
    return lax.ppermute(array, "probe", [(0, 1), (1, 0)])


def body(features, probes, lengthscale, near_blocks, leaf_order):
    blocks = near_blocks.shape[0]
    me = lax.axis_index("probe").astype(jnp.int32)[None]
    first = ((lax.axis_index("leaf") - 1) * blocks).astype(jnp.int32)[None]
    probes_before = beside(probes, 1)
    probes_after = beside(probes, -1)
    ordered = order_features(features, leaf_order)
    part, rows_t, far, weight = near_part(near_blocks, first, lengthscale, ordered, probes)
    sent, part = lax.optimization_barrier((ordered, part))
    before = beside(sent, 1)
    after = beside(sent, -1)
    own = far_part(
        far, weight, part, rows_t, before, after, probes_before, probes_after, blocks
    )
    other = other_core(own)
    block, high, low = own_gram(own)
    gram, highs, lows = gram_blocks(me, block, high, low, other)
    grams = [gram]
    for flip in (1, 2, 7, 8):
        gram = gram + sibling(gram, flip)
        grams.append(gram)
    mine = jnp.concatenate(grams, 0)
    return factors(me, mine, other_core(mine), highs, lows)


def solution(mesh):
    in_specs = (P(None, "leaf"), P("probe", "leaf"), P(), P("leaf", None), P("leaf", None))
    out_specs = (P(None, "leaf", "probe"), P("leaf", "probe"))
    return jax.shard_map(body, mesh=mesh, in_specs=in_specs, out_specs=out_specs, check_vma=False)
```

```python
import math

import jax
import jax.numpy as jnp
from jax import lax
from jax.experimental import pallas as pl
from jax.experimental.pallas import tpu as pltpu
from jax.sharding import PartitionSpec as P

LEVELS = 4
LANES = 128
ROWS = 8
TILE = (ROWS, LANES)
LOG2_E = 1.4426950408889634
LN_2 = 0.6931471805599453
NUGGET = 2.0
TINY = 1e-20
HI = lax.Precision.HIGHEST
F32 = jnp.float32
BF16 = jnp.bfloat16
VMEM_BYTES = 14 << 20


def call(kernel, out_shape, **kwargs):
    return pl.pallas_call(
        kernel,
        out_shape=out_shape,
        compiler_params=pltpu.CompilerParams(vmem_limit_bytes=VMEM_BYTES),
        **kwargs,
    )


def dot(a, b, ca, cb, precision=HI):
    return lax.dot_general(
        a, b, (((ca,), (cb,)), ((), ())), precision=precision, preferred_element_type=F32
    )


def dot16(a, b, ca, cb):
    return lax.dot_general(a, b, (((ca,), (cb,)), ((), ())), preferred_element_type=F32)


def halves(x):
    hi = x.astype(BF16)
    return hi, (x - hi.astype(F32)).astype(BF16)


def thirds(x):
    hi = x.astype(BF16).astype(F32)
    rest = x - hi
    mid = rest.astype(BF16).astype(F32)
    return hi, mid, rest - mid


def in_hbm(array):
    return pltpu.with_memory_space_constraint(array, pltpu.HBM)


def order_kernel(feat_in, order_in, out, feat, order, sems):
    copies = [
        pltpu.make_async_copy(feat_in, feat, sems.at[0]),
        pltpu.make_async_copy(order_in, order, sems.at[1]),
    ]
    for copy in copies:
        copy.start()
    for copy in copies:
        copy.wait()
    chunks = feat.shape[1] // LANES
    pieces = [feat[:, c * LANES : (c + 1) * LANES].astype(F32) for c in range(chunks)]

    def one(q, carry):
        at = pl.multiple_of(q * LANES, LANES)
        index = jnp.broadcast_to(order[:, pl.ds(at, LANES)], TILE)
        low, high = index & (LANES - 1), index >> 7
        total = jnp.zeros(TILE, F32)
        for c in range(chunks):
            total = jnp.where(high == c, jnp.take_along_axis(pieces[c], low, axis=1), total)
        out[:, pl.ds(at, LANES)] = total.astype(BF16)
        return carry

    lax.fori_loop(0, chunks, one, 0, unroll=chunks)


def order_features(features, leaf_order):
    anywhere = pl.BlockSpec(memory_space=pltpu.HBM)
    return call(
        order_kernel,
        jax.ShapeDtypeStruct(features.shape, BF16),
        in_specs=[anywhere] * 2,
        out_specs=pl.BlockSpec(memory_space=pltpu.VMEM),
        scratch_shapes=[
            pltpu.VMEM(features.shape, BF16),
            pltpu.VMEM(leaf_order.shape, jnp.int32),
            pltpu.SemaphoreType.DMA((2,)),
        ],
    )(in_hbm(features), in_hbm(leaf_order))


SHIFT = 6
SLOTS = 160
WIDE = 4


def column_pieces(x, weight):
    norm = jnp.sum(x * x * weight, 0, keepdims=True)
    ones = jnp.ones_like(norm)
    zeros = jnp.zeros((2, x.shape[1]), F32)
    return jnp.concatenate([x, x, x, *thirds(norm), ones, ones, ones, zeros], 0).astype(BF16)


def row_pieces(x, weight):
    norm = jnp.sum(x * x * weight, 0, keepdims=True)
    ones = jnp.ones_like(norm)
    zeros = jnp.zeros((2, x.shape[1]), F32)
    return jnp.concatenate(
        [*thirds(-2.0 * weight * x), ones, ones, ones, *thirds(norm), zeros], 0
    ).T.astype(BF16)


def weights(scale):
    count = scale.shape[0]
    row = lax.broadcasted_iota(jnp.int32, (count, LANES), 0)
    held = jnp.full((count, LANES), scale[0], F32)
    for f in range(1, count):
        held = jnp.where(row == f, scale[f], held)
    return (3.0 * LOG2_E * LOG2_E) / (held * held)


def load_columns(cols, panel, feats, weight, blocks):
    block = feats[0].shape[1] // blocks
    for n, feat in enumerate(feats):
        pieces = column_pieces(feat[...].astype(F32), weight)
        for b in range(blocks):
            cols[n * blocks + b] = pieces[:, b * block : (b + 1) * block]
    last = len(feats) * blocks
    cols[last] = jnp.zeros(cols.shape[1:], BF16)
    panel[last] = jnp.zeros(panel.shape[1:], BF16)


def run_tasks(tasks, count, slot_of, rows_t, cols, panel, out, kerns):
    block = cols.shape[2]

    def where_of(n):
        code = tasks[n]
        at = pl.ds(pl.multiple_of((code >> SHIFT) * block, block), block)
        return at, slot_of(code & ((1 << SHIFT) - 1))

    def product(n, kern):
        at, slot = where_of(n)
        return at, dot16(kern, panel[slot], 1, 1)

    def some(i, carry):
        for half in range(2):
            group = 2 * i + half
            last = jnp.maximum(group - 1, 0)
            for u in range(WIDE):
                to, part = product(last * WIDE + u, kerns[1 - half][u])
                at, slot = where_of(group * WIDE + u)
                dist = jnp.maximum(dot16(rows_t[at, :], cols[slot], 1, 0), TINY)
                root = dist * lax.rsqrt(dist)
                kerns[half][u] = ((1.0 + LN_2 * root) * jnp.exp2(-root)).astype(BF16)
                out[to, :] += part
        return carry

    kerns[1][...] = jnp.zeros_like(kerns[1])
    pairs = (count + (2 * WIDE - 1)) // (2 * WIDE)
    lax.fori_loop(0, pairs, some, 0)
    for u in range(WIDE):
        to, part = product(jnp.maximum(2 * pairs - 1, 0) * WIDE + u, kerns[1][u])
        out[to, :] += part


def near_kernel(
    first, listed_in, scale_in, feat, probes, out, rows_t, far, weight_out,
    near_blocks, scale, tasks, cols, panel, k0, k1, sems,
):
    blocks, near = near_blocks.shape
    block = feat.shape[1] // blocks
    copies = [
        pltpu.make_async_copy(listed_in, near_blocks, sems.at[0]),
        pltpu.make_async_copy(scale_in, scale, sems.at[1]),
    ]
    for b in range(blocks):
        source = probes.at[:, b * block : (b + 1) * block]
        copies.append(pltpu.make_async_copy(source, panel.at[b], sems.at[2 + b]))
    for copy in copies:
        copy.start()
    copies[0].wait()

    def scan(a, counts):
        mine, rest = counts
        for j in range(near):
            listed = near_blocks[a, j] - first[0]
            code = (a << SHIFT) + listed
            inside = jnp.where((listed >= blocks) & (listed < 2 * blocks), 1, 0)
            tasks[mine] = code
            far[rest] = code
            mine = mine + inside
            rest = rest + (1 - inside)
        return mine, rest

    mine, rest = lax.fori_loop(0, blocks, scan, (jnp.int32(0), jnp.int32(0)))
    for u in range(2 * WIDE):
        tasks[mine + u] = 2 * blocks
        far[rest + u] = 3 * blocks
    far[SLOTS - 1] = rest

    copies[1].wait()
    weight_out[...] = weights(scale)
    weight = weight_out[:, :1]
    rows_t[...] = row_pieces(feat[...].astype(F32), weight)
    load_columns(cols, panel, [feat], weight, blocks)
    for copy in copies[2:]:
        copy.wait()
    here = lax.broadcasted_iota(jnp.int32, (block, block), 0)
    there = lax.broadcasted_iota(jnp.int32, (block, block), 1)
    nugget = jnp.where(here == there, NUGGET, 0.0).astype(BF16)
    for b in range(blocks):
        out[b * block : (b + 1) * block, :] = dot16(nugget, panel[b], 1, 1)
    run_tasks(tasks, mine, lambda listed: listed - blocks, rows_t, cols, panel, out, (k0, k1))


def near_part(near_blocks, first, scale, feat, probes):
    half, leaf = probes.shape
    blocks = near_blocks.shape[0]
    block = leaf // blocks
    whole = pl.BlockSpec(memory_space=pltpu.VMEM)
    anywhere = pl.BlockSpec(memory_space=pltpu.HBM)
    return call(
        near_kernel,
        (
            pltpu.VMEM((leaf, half), F32),
            pltpu.VMEM((leaf, 32), BF16),
            jax.ShapeDtypeStruct((SLOTS,), jnp.int32),
            pltpu.VMEM((ROWS, LANES), F32),
        ),
        grid_spec=pltpu.PrefetchScalarGridSpec(
            num_scalar_prefetch=1,
            grid=(1,),
            in_specs=[anywhere, anywhere, whole, anywhere],
            out_specs=[whole, whole, pl.BlockSpec(memory_space=pltpu.SMEM), whole],
            scratch_shapes=[
                pltpu.SMEM(near_blocks.shape, jnp.int32),
                pltpu.SMEM(scale.shape, F32),
                pltpu.SMEM((SLOTS,), jnp.int32),
                pltpu.VMEM((blocks + 1, 32, block), BF16),
                pltpu.VMEM((blocks + 1, half, block), BF16),
                *[pltpu.VMEM((WIDE, block, block), BF16)] * 2,
                pltpu.SemaphoreType.DMA((2 + blocks,)),
            ],
        ),
    )(first, in_hbm(near_blocks), in_hbm(scale), feat, in_hbm(probes))


def far_kernel(far, weight, part, rows_t, left, right, before, after, out, cols, panel, k0, k1):
    blocks = (cols.shape[0] - 1) // 2
    load_columns(cols, panel, [left, right], weight[:, :1], blocks)
    block = cols.shape[2]
    for n, probe in enumerate((before, after)):
        for b in range(blocks):
            panel[n * blocks + b] = probe[:, b * block : (b + 1) * block]
    out[...] = part[...]
    run_tasks(
        far,
        far[SLOTS - 1],
        lambda listed: jnp.where(listed < blocks, listed, listed - blocks),
        rows_t,
        cols,
        panel,
        out,
        (k0, k1),
    )


def far_part(far, weight, part, rows_t, left, right, before, after, blocks):
    half, leaf = before.shape
    block = leaf // blocks
    whole = pl.BlockSpec(memory_space=pltpu.VMEM)
    return call(
        far_kernel,
        pltpu.VMEM((leaf, half), F32),
        grid_spec=pltpu.PrefetchScalarGridSpec(
            num_scalar_prefetch=1,
            grid=(1,),
            in_specs=[whole] * 7,
            out_specs=whole,
            scratch_shapes=[
                pltpu.VMEM((2 * blocks + 1, 32, block), BF16),
                pltpu.VMEM((2 * blocks + 1, half, block), BF16),
                *[pltpu.VMEM((WIDE, block, block), BF16)] * 2,
            ],
        ),
    )(far, weight, part, rows_t, left, right, before, after)


HALF = LANES // 2
PACKED = HALF + ROWS


def pack(block):
    shape = (HALF, LANES)
    row = lax.broadcasted_iota(jnp.int32, shape, 0)
    col = lax.broadcasted_iota(jnp.int32, shape, 1) - HALF
    bottom = block[HALF:, :]
    top = pltpu.roll(block[:HALF, :], HALF, 1)
    diagonal = jnp.sum(jnp.where(row == col, bottom, 0.0), 0, keepdims=True)
    body = jnp.where((col >= 0) & (row >= col), top, bottom)
    return body, jnp.broadcast_to(diagonal, TILE)


def unpack(body, diagonal):
    shape = (HALF, HALF)
    row = lax.broadcasted_iota(jnp.int32, shape, 0)
    col = lax.broadcasted_iota(jnp.int32, shape, 1)
    side = body[:, :HALF]
    fold = body[:, HALF:]
    flip = fold.T
    top = jnp.where(row >= col, fold, flip)
    bottom = jnp.where(row < col, fold, flip)
    bottom = jnp.where(row == col, diagonal[:1, HALF:], bottom)
    return jnp.concatenate(
        [jnp.concatenate([top, side.T], 1), jnp.concatenate([side, bottom], 1)], 0
    )


def product(a, b):
    return dot16(a[0], b[0], 0, 0) + (dot16(a[0], b[1], 0, 0) + dot16(a[1], b[0], 0, 0))


def own_kernel(own, out, high, low):
    a0, a1 = halves(own[...])
    high[:, :LANES] = a0
    low[:, :LANES] = a1
    out[:HALF], out[HALF:] = pack(product((a0, a1), (a0, a1)))


def own_gram(own):
    leaf, half = own.shape
    return call(
        own_kernel,
        (
            pltpu.VMEM((PACKED, half), F32),
            pltpu.VMEM((leaf, 2 * half), BF16),
            pltpu.VMEM((leaf, 2 * half), BF16),
        ),
    )(own)


def gram_kernel(me, block, high, low, other, out, highs, lows):
    n = LANES
    b0, b1 = halves(other[...])
    a0, a1 = high.at[:, :n], low.at[:, :n]
    highs[:, n:] = b0
    lows[:, n:] = b1
    out[:PACKED] = block[...]

    @pl.when(me[0] == 0)
    def _():
        out[PACKED:] = product((b0[:, :HALF], b1[:, :HALF]), (a0[...], a1[...]))

    @pl.when(me[0] == 1)
    def _():
        out[PACKED:] = product((high[:, HALF:n], low[:, HALF:n]), (b0, b1))


def gram_blocks(me, block, high, low, other):
    leaf, half = other.shape
    whole = pl.BlockSpec(memory_space=pltpu.VMEM)
    return call(
        gram_kernel,
        (
            jax.ShapeDtypeStruct((PACKED + HALF, half), F32),
            pltpu.VMEM((leaf, 2 * half), BF16),
            pltpu.VMEM((leaf, 2 * half), BF16),
        ),
        grid_spec=pltpu.PrefetchScalarGridSpec(
            num_scalar_prefetch=1, grid=(1,), in_specs=[whole] * 4, out_specs=[whole] * 3
        ),
        input_output_aliases={2: 1, 3: 2},
    )(me, block, high, low, other)


def row_of(x, k):
    return jnp.broadcast_to(x[k : k + 1, :], TILE)


def columns(panel, at):
    return [
        jnp.take_along_axis(panel, jnp.full(TILE, at + m, jnp.int32), axis=1)
        for m in range(ROWS)
    ]


def outer_pieces(a, b):
    a0, a1, a2 = thirds(a)
    b0, b1, b2 = thirds(b)
    left = jnp.concatenate([a0, a0, a1, a0, a1, a2], 0).astype(BF16)
    right = jnp.concatenate([b0, b1, b0, b2, b1, b0], 0).astype(BF16)
    return left, right


def eliminate(panels, nexts, at):
    count = range(len(panels))
    lane = lax.broadcasted_iota(jnp.int32, TILE, 1)
    sub = lax.broadcasted_iota(jnp.int32, TILE, 0)
    here = (lane >= at) & (lane < at + ROWS)
    unit = jnp.where(lane - at == sub, 1.0, 0.0)
    cols = [columns(panels[l], at) for l in count]
    rows = [jnp.where(here, unit, panels[l]) for l in count]
    lows = [jnp.zeros(TILE, F32) for l in count]
    below = [columns(panel, at) for panel in nexts]
    nexts = [jnp.where(here, 0.0, panel) for panel in nexts]
    for k in range(ROWS):
        inv = [lax.rsqrt(row_of(cols[l][k], k)) for l in count]
        low = [jnp.where(sub >= k, cols[l][k] * inv[l], 0.0) for l in count]
        for l in count:
            lead = row_of(rows[l], k) * inv[l]
            rows[l] = jnp.where(sub == k, lead, rows[l] - low[l] * lead)
            lows[l] = jnp.where(lane == at + k, low[l], lows[l])
            if nexts:
                below[l][k] = below[l][k] * inv[l]
                nexts[l] = nexts[l] - below[l][k] * lead
        for m in range(k + 1, ROWS):
            for l in count:
                one = row_of(low[l], m)
                cols[l][m] = cols[l][m] - low[l] * one
                if nexts:
                    below[l][m] = below[l][m] - below[l][k] * one
    return rows, lows, nexts


def factor_block(work, ups, invs, base):
    count = range(work.shape[0])
    lane = lax.broadcasted_iota(jnp.int32, TILE, 1)
    span = slice(base, base + LANES)
    pair = 2 * ROWS
    for at in range(0, LANES, pair):
        mid, end = at + ROWS, at + pair
        both = [work[l, at:end, :] for l in count]
        first, low_first, second = eliminate(
            [b[:ROWS] for b in both], [b[ROWS:] for b in both], at
        )
        second, low_second, _ = eliminate(second, [], mid)
        for l in count:
            for x, low, p in ((first, low_first, at), (second, low_second, mid)):
                to = slice(base + p, base + p + ROWS)
                ups[l, to, span] = jnp.where(lane >= p + ROWS, x[l], low[l])
                invs[l, to, span] = jnp.where(lane < p + ROWS, x[l], 0.0)
        if end == LANES:
            break
        lefts, rights = [], []
        for l in count:
            lefts.append(jnp.concatenate([first[l], second[l]], 0))
            rights.append(
                jnp.concatenate(
                    [jnp.where((lane >= mid) & (lane < end), 0.0, first[l]), second[l]], 0
                )
            )
        pieces = [outer_pieces(lefts[l], rights[l]) for l in count]
        col = lax.broadcasted_iota(jnp.int32, (LANES - end, LANES), 1)
        gone = (col >= at) & (col < end)
        sums = [dot16(pieces[l][0][:, end:], pieces[l][1], 0, 0) for l in count]
        for l in count:
            work[l, end:, :] = jnp.where(gone, 0.0, work[l, end:, :]) - sums[l]


def straighten(ups, l, base):
    n = LANES
    block = ups[l, base : base + n, base : base + n]
    row = lax.broadcasted_iota(jnp.int32, (n, n), 0)
    col = lax.broadcasted_iota(jnp.int32, (n, n), 1)
    ups[l, base : base + n, base : base + n] = jnp.where(row >> 3 == col >> 3, block.T, block)


def factor(grams, work, ups, invs):
    n = LANES
    blank = jnp.zeros((n, n), F32)
    count = range(work.shape[0])
    for l in count:
        work[l] = grams(l, 0)
    factor_block(work, ups, invs, 0)
    sides = [dot(invs[l, 0:n, 0:n], grams(l, 1), 1, 1) for l in count]
    for l in count:
        ups[l, 0:n, n : 2 * n] = sides[l]
        ups[l, n : 2 * n, 0:n] = blank
        invs[l, 0:n, n : 2 * n] = blank
    squares = [dot(sides[l], sides[l], 0, 0) for l in count]
    for l in count:
        work[l] = grams(l, 2) - squares[l]
    factor_block(work, ups, invs, n)
    downs = [dot(ups[l, 0:n, n : 2 * n], invs[l, 0:n, 0:n], 0, 0) for l in count]
    downs = [dot(invs[l, n : 2 * n, n : 2 * n], downs[l], 1, 0) for l in count]
    for l in count:
        invs[l, n : 2 * n, 0:n] = -downs[l]
        straighten(ups, l, 0)
        straighten(ups, l, n)


def factor_kernel(
    me, mine, theirs, highs, lows, transfer, basis, pieces, work, ups, invs, moved, rows, sems
):
    n = LANES
    height = PACKED + HALF
    pieces[me[0]] = mine[...]
    pieces[1 - me[0]] = theirs[...]

    def gram(l, b):
        at = l * height
        if b == 1:
            return jnp.concatenate([pieces[p, at + PACKED : at + height, :] for p in range(2)], 0)
        part = pieces.at[b // 2]
        return unpack(part[at : at + HALF, :], part[at + HALF : at + PACKED, :])

    factor(gram, work, ups, invs)
    cols = pl.ds(pl.multiple_of(me[0] * n, n), n)
    rest = pl.ds(pl.multiple_of((1 - me[0]) * n, n), n)
    scale = math.sqrt(2**LEVELS * highs.shape[0])
    weight = invs.at[LEVELS]
    high, low = halves(jnp.concatenate([weight[cols, cols], weight[cols, rest]], 1) * scale)
    both = jnp.concatenate([high, low], 0)
    steps, size, _ = rows.shape
    copies = []
    for s in range(steps):
        at = slice(s * size, (s + 1) * size)
        two = dot16(highs[at, :], both, 1, 1)
        rows[s] = two[:, :n] + (two[:, n:] + dot16(lows[at, :], high, 1, 1))
        copies.append(pltpu.make_async_copy(rows.at[s], basis.at[pl.ds(s * size, size)], sems.at[s]))
        copies[-1].start()
    for l in range(LEVELS):
        moved[l] = dot(ups[l], invs[l + 1, cols, :], 1, 1)
        copies.append(pltpu.make_async_copy(moved.at[l], transfer.at[l], sems.at[steps + l]))
        copies[-1].start()
    for copy in copies:
        copy.wait()


def factors(me, mine, theirs, highs, lows):
    n = 2 * LANES
    count = LEVELS + 1
    leaf, half = highs.shape[0], LANES
    steps = 6
    whole = pl.BlockSpec(memory_space=pltpu.VMEM)
    return call(
        factor_kernel,
        (
            jax.ShapeDtypeStruct((LEVELS, n, half), F32),
            jax.ShapeDtypeStruct((leaf, half), F32),
        ),
        grid_spec=pltpu.PrefetchScalarGridSpec(
            num_scalar_prefetch=1,
            grid=(1,),
            in_specs=[whole] * 4,
            out_specs=[pl.BlockSpec(memory_space=pl.ANY)] * 2,
            scratch_shapes=[
                pltpu.VMEM((2, *mine.shape), F32),
                pltpu.VMEM((count, LANES, LANES), F32),
                pltpu.VMEM((count, n, n), F32),
                pltpu.VMEM((count, n, n), F32),
                pltpu.VMEM((LEVELS, n, half), F32),
                pltpu.VMEM((steps, leaf // steps, half), F32),
                pltpu.SemaphoreType.DMA((steps + LEVELS,)),
            ],
        ),
    )(me, mine, theirs, highs, lows)


def beside(array, shift):
    count = lax.axis_size("leaf")
    pairs = [(i, i + shift) for i in range(count) if 0 <= i + shift < count]
    return lax.ppermute(array, "leaf", pairs)


def sibling(array, flip):
    return lax.ppermute(array, "leaf", [(i, i ^ flip) for i in range(lax.axis_size("leaf"))])


def other_core(array):
    return lax.ppermute(array, "probe", [(0, 1), (1, 0)])


def body(features, probes, lengthscale, near_blocks, leaf_order):
    blocks = near_blocks.shape[0]
    me = lax.axis_index("probe").astype(jnp.int32)[None]
    first = ((lax.axis_index("leaf") - 1) * blocks).astype(jnp.int32)[None]
    probes_before = beside(probes, 1)
    probes_after = beside(probes, -1)
    ordered = order_features(features, leaf_order)
    before = beside(ordered, 1)
    after = beside(ordered, -1)
    part, rows_t, far, weight = near_part(near_blocks, first, lengthscale, ordered, probes)
    own = far_part(
        far, weight, part, rows_t, before, after, probes_before, probes_after, blocks
    )
    other = other_core(own)
    block, high, low = own_gram(own)
    gram, highs, lows = gram_blocks(me, block, high, low, other)
    grams = [gram]
    for flip in (1, 2, 7, 8):
        gram = gram + sibling(gram, flip)
        grams.append(gram)
    mine = jnp.concatenate(grams, 0)
    return factors(me, mine, other_core(mine), highs, lows)


def solution(mesh):
    in_specs = (P(None, "leaf"), P("probe", "leaf"), P(), P("leaf", None), P("leaf", None))
    out_specs = (P(None, "leaf", "probe"), P("leaf", "probe"))
    return jax.shard_map(body, mesh=mesh, in_specs=in_specs, out_specs=out_specs, check_vma=False)
```

```python
import math

import jax
import jax.numpy as jnp
from jax import lax
from jax.experimental import pallas as pl
from jax.experimental.pallas import tpu as pltpu
from jax.sharding import PartitionSpec as P

LEVELS = 4
LANES = 128
ROWS = 8
TILE = (ROWS, LANES)
LOG2_E = 1.4426950408889634
LN_2 = 0.6931471805599453
NUGGET = 2.0
TINY = 1e-20
HI = lax.Precision.HIGHEST
F32 = jnp.float32
BF16 = jnp.bfloat16
VMEM_BYTES = 14 << 20


def call(kernel, out_shape, **kwargs):
    return pl.pallas_call(
        kernel,
        out_shape=out_shape,
        compiler_params=pltpu.CompilerParams(vmem_limit_bytes=VMEM_BYTES),
        **kwargs,
    )


def dot(a, b, ca, cb, precision=HI):
    return lax.dot_general(
        a, b, (((ca,), (cb,)), ((), ())), precision=precision, preferred_element_type=F32
    )


def dot16(a, b, ca, cb):
    return lax.dot_general(a, b, (((ca,), (cb,)), ((), ())), preferred_element_type=F32)


def halves(x):
    hi = x.astype(BF16)
    return hi, (x - hi.astype(F32)).astype(BF16)


def thirds(x):
    hi = x.astype(BF16).astype(F32)
    rest = x - hi
    mid = rest.astype(BF16).astype(F32)
    return hi, mid, rest - mid


def in_hbm(array):
    return pltpu.with_memory_space_constraint(array, pltpu.HBM)


def order_kernel(feat_in, order_in, probes_in, out, feat, order, sems):
    rows = probes_in.shape[0]
    moved = pltpu.make_async_copy(probes_in, out.at[:rows], sems.at[2])
    moved.start()
    copies = [
        pltpu.make_async_copy(feat_in, feat, sems.at[0]),
        pltpu.make_async_copy(order_in, order, sems.at[1]),
    ]
    for copy in copies:
        copy.start()
    for copy in copies:
        copy.wait()
    chunks = feat.shape[1] // LANES
    pieces = [feat[:, c * LANES : (c + 1) * LANES].astype(F32) for c in range(chunks)]

    def one(q, carry):
        at = pl.multiple_of(q * LANES, LANES)
        index = jnp.broadcast_to(order[:, pl.ds(at, LANES)], TILE)
        low, high = index & (LANES - 1), index >> 7
        total = jnp.zeros(TILE, F32)
        for c in range(chunks):
            total = jnp.where(high == c, jnp.take_along_axis(pieces[c], low, axis=1), total)
        out[rows:, pl.ds(at, LANES)] = total.astype(BF16)
        return carry

    lax.fori_loop(0, chunks, one, 0, unroll=chunks)
    moved.wait()


def order_features(features, leaf_order, probes):
    anywhere = pl.BlockSpec(memory_space=pltpu.HBM)
    return call(
        order_kernel,
        jax.ShapeDtypeStruct((probes.shape[0] + features.shape[0], features.shape[1]), BF16),
        in_specs=[anywhere] * 3,
        out_specs=pl.BlockSpec(memory_space=pltpu.VMEM),
        scratch_shapes=[
            pltpu.VMEM(features.shape, BF16),
            pltpu.VMEM(leaf_order.shape, jnp.int32),
            pltpu.SemaphoreType.DMA((3,)),
        ],
    )(in_hbm(features), in_hbm(leaf_order), in_hbm(probes))


SHIFT = 6
SLOTS = 160
WIDE = 4


def column_pieces(x, weight):
    norm = jnp.sum(x * x * weight, 0, keepdims=True)
    ones = jnp.ones_like(norm)
    zeros = jnp.zeros((2, x.shape[1]), F32)
    return jnp.concatenate([x, x, x, *thirds(norm), ones, ones, ones, zeros], 0).astype(BF16)


def row_pieces(x, weight):
    norm = jnp.sum(x * x * weight, 0, keepdims=True)
    ones = jnp.ones_like(norm)
    zeros = jnp.zeros((2, x.shape[1]), F32)
    return jnp.concatenate(
        [*thirds(-2.0 * weight * x), ones, ones, ones, *thirds(norm), zeros], 0
    ).T.astype(BF16)


def weights(scale):
    count = scale.shape[0]
    row = lax.broadcasted_iota(jnp.int32, (count, LANES), 0)
    held = jnp.full((count, LANES), scale[0], F32)
    for f in range(1, count):
        held = jnp.where(row == f, scale[f], held)
    return (3.0 * LOG2_E * LOG2_E) / (held * held)


def load_columns(cols, panel, feats, weight, blocks):
    block = feats[0].shape[1] // blocks
    for n, feat in enumerate(feats):
        pieces = column_pieces(feat[...].astype(F32), weight)
        for b in range(blocks):
            cols[n * blocks + b] = pieces[:, b * block : (b + 1) * block]
    last = len(feats) * blocks
    cols[last] = jnp.zeros(cols.shape[1:], BF16)
    panel[last] = jnp.zeros(panel.shape[1:], BF16)


def run_tasks(tasks, count, slot_of, rows_t, cols, panel, out, kerns):
    block = cols.shape[2]

    def where_of(n):
        code = tasks[n]
        at = pl.ds(pl.multiple_of((code >> SHIFT) * block, block), block)
        return at, slot_of(code & ((1 << SHIFT) - 1))

    def product(n, kern):
        at, slot = where_of(n)
        return at, dot16(kern, panel[slot], 1, 1)

    def some(i, carry):
        for half in range(2):
            group = 2 * i + half
            last = jnp.maximum(group - 1, 0)
            for u in range(WIDE):
                to, part = product(last * WIDE + u, kerns[1 - half][u])
                at, slot = where_of(group * WIDE + u)
                dist = jnp.maximum(dot16(rows_t[at, :], cols[slot], 1, 0), TINY)
                root = dist * lax.rsqrt(dist)
                kerns[half][u] = ((1.0 + LN_2 * root) * jnp.exp2(-root)).astype(BF16)
                out[to, :] += part
        return carry

    kerns[1][...] = jnp.zeros_like(kerns[1])
    pairs = (count + (2 * WIDE - 1)) // (2 * WIDE)
    lax.fori_loop(0, pairs, some, 0)
    for u in range(WIDE):
        to, part = product(jnp.maximum(2 * pairs - 1, 0) * WIDE + u, kerns[1][u])
        out[to, :] += part


def near_kernel(
    first, listed_in, scale_in, stack, probes, out, rows_t, far, weight_out,
    near_blocks, scale, tasks, cols, panel, k0, k1, sems,
):
    blocks, near = near_blocks.shape
    feat = stack.at[probes.shape[0] :]
    block = feat.shape[1] // blocks
    copies = [
        pltpu.make_async_copy(listed_in, near_blocks, sems.at[0]),
        pltpu.make_async_copy(scale_in, scale, sems.at[1]),
    ]
    for b in range(blocks):
        source = probes.at[:, b * block : (b + 1) * block]
        copies.append(pltpu.make_async_copy(source, panel.at[b], sems.at[2 + b]))
    for copy in copies:
        copy.start()
    copies[0].wait()

    def scan(a, counts):
        mine, rest = counts
        for j in range(near):
            listed = near_blocks[a, j] - first[0]
            code = (a << SHIFT) + listed
            inside = jnp.where((listed >= blocks) & (listed < 2 * blocks), 1, 0)
            tasks[mine] = code
            far[rest] = code
            mine = mine + inside
            rest = rest + (1 - inside)
        return mine, rest

    mine, rest = lax.fori_loop(0, blocks, scan, (jnp.int32(0), jnp.int32(0)))
    for u in range(2 * WIDE):
        tasks[mine + u] = 2 * blocks
        far[rest + u] = 3 * blocks
    far[SLOTS - 1] = rest

    copies[1].wait()
    weight_out[...] = weights(scale)
    weight = weight_out[:, :1]
    rows_t[...] = row_pieces(feat[...].astype(F32), weight)
    load_columns(cols, panel, [feat], weight, blocks)
    for copy in copies[2:]:
        copy.wait()
    here = lax.broadcasted_iota(jnp.int32, (block, block), 0)
    there = lax.broadcasted_iota(jnp.int32, (block, block), 1)
    nugget = jnp.where(here == there, NUGGET, 0.0).astype(BF16)
    for b in range(blocks):
        out[b * block : (b + 1) * block, :] = dot16(nugget, panel[b], 1, 1)
    run_tasks(tasks, mine, lambda listed: listed - blocks, rows_t, cols, panel, out, (k0, k1))


def near_part(near_blocks, first, scale, feat, probes):
    half, leaf = probes.shape
    blocks = near_blocks.shape[0]
    block = leaf // blocks
    whole = pl.BlockSpec(memory_space=pltpu.VMEM)
    anywhere = pl.BlockSpec(memory_space=pltpu.HBM)
    return call(
        near_kernel,
        (
            pltpu.VMEM((leaf, half), F32),
            pltpu.VMEM((leaf, 32), BF16),
            jax.ShapeDtypeStruct((SLOTS,), jnp.int32),
            pltpu.VMEM((ROWS, LANES), F32),
        ),
        grid_spec=pltpu.PrefetchScalarGridSpec(
            num_scalar_prefetch=1,
            grid=(1,),
            in_specs=[anywhere, anywhere, whole, anywhere],
            out_specs=[whole, whole, pl.BlockSpec(memory_space=pltpu.SMEM), whole],
            scratch_shapes=[
                pltpu.SMEM(near_blocks.shape, jnp.int32),
                pltpu.SMEM(scale.shape, F32),
                pltpu.SMEM((SLOTS,), jnp.int32),
                pltpu.VMEM((blocks + 1, 32, block), BF16),
                pltpu.VMEM((blocks + 1, half, block), BF16),
                *[pltpu.VMEM((WIDE, block, block), BF16)] * 2,
                pltpu.SemaphoreType.DMA((2 + blocks,)),
            ],
        ),
    )(first, in_hbm(near_blocks), in_hbm(scale), feat, in_hbm(probes))


def far_kernel(far, weight, part, rows_t, before, after, out, cols, panel, k0, k1):
    blocks = (cols.shape[0] - 1) // 2
    rows = panel.shape[1]
    left, right = before.at[rows:], after.at[rows:]
    load_columns(cols, panel, [left, right], weight[:, :1], blocks)
    block = cols.shape[2]
    for n, probe in enumerate((before, after)):
        for b in range(blocks):
            panel[n * blocks + b] = probe[:rows, b * block : (b + 1) * block]
    out[...] = part[...]
    run_tasks(
        far,
        far[SLOTS - 1],
        lambda listed: jnp.where(listed < blocks, listed, listed - blocks),
        rows_t,
        cols,
        panel,
        out,
        (k0, k1),
    )


def far_part(far, weight, part, rows_t, before, after, blocks):
    leaf, half = part.shape
    block = leaf // blocks
    whole = pl.BlockSpec(memory_space=pltpu.VMEM)
    return call(
        far_kernel,
        pltpu.VMEM((leaf, half), F32),
        grid_spec=pltpu.PrefetchScalarGridSpec(
            num_scalar_prefetch=1,
            grid=(1,),
            in_specs=[whole] * 5,
            out_specs=whole,
            scratch_shapes=[
                pltpu.VMEM((2 * blocks + 1, 32, block), BF16),
                pltpu.VMEM((2 * blocks + 1, half, block), BF16),
                *[pltpu.VMEM((WIDE, block, block), BF16)] * 2,
            ],
        ),
    )(far, weight, part, rows_t, before, after)


HALF = LANES // 2
PACKED = HALF + ROWS


def pack(block):
    shape = (HALF, LANES)
    row = lax.broadcasted_iota(jnp.int32, shape, 0)
    col = lax.broadcasted_iota(jnp.int32, shape, 1) - HALF
    bottom = block[HALF:, :]
    top = pltpu.roll(block[:HALF, :], HALF, 1)
    diagonal = jnp.sum(jnp.where(row == col, bottom, 0.0), 0, keepdims=True)
    body = jnp.where((col >= 0) & (row >= col), top, bottom)
    return body, jnp.broadcast_to(diagonal, TILE)


def unpack(body, diagonal):
    shape = (HALF, HALF)
    row = lax.broadcasted_iota(jnp.int32, shape, 0)
    col = lax.broadcasted_iota(jnp.int32, shape, 1)
    side = body[:, :HALF]
    fold = body[:, HALF:]
    flip = fold.T
    top = jnp.where(row >= col, fold, flip)
    bottom = jnp.where(row < col, fold, flip)
    bottom = jnp.where(row == col, diagonal[:1, HALF:], bottom)
    return jnp.concatenate(
        [jnp.concatenate([top, side.T], 1), jnp.concatenate([side, bottom], 1)], 0
    )


def product(a, b):
    return dot16(a[0], b[0], 0, 0) + (dot16(a[0], b[1], 0, 0) + dot16(a[1], b[0], 0, 0))


def own_kernel(own, out, high, low):
    a0, a1 = halves(own[...])
    high[:, :LANES] = a0
    low[:, :LANES] = a1
    out[:HALF], out[HALF:] = pack(product((a0, a1), (a0, a1)))


def own_gram(own):
    leaf, half = own.shape
    return call(
        own_kernel,
        (
            pltpu.VMEM((PACKED, half), F32),
            pltpu.VMEM((leaf, 2 * half), BF16),
            pltpu.VMEM((leaf, 2 * half), BF16),
        ),
    )(own)


def gram_kernel(me, block, high, low, other, out, highs, lows):
    n = LANES
    b0, b1 = halves(other[...])
    a0, a1 = high.at[:, :n], low.at[:, :n]
    highs[:, n:] = b0
    lows[:, n:] = b1
    out[:PACKED] = block[...]

    @pl.when(me[0] == 0)
    def _():
        out[PACKED:] = product((b0[:, :HALF], b1[:, :HALF]), (a0[...], a1[...]))

    @pl.when(me[0] == 1)
    def _():
        out[PACKED:] = product((high[:, HALF:n], low[:, HALF:n]), (b0, b1))


def gram_blocks(me, block, high, low, other):
    leaf, half = other.shape
    whole = pl.BlockSpec(memory_space=pltpu.VMEM)
    return call(
        gram_kernel,
        (
            jax.ShapeDtypeStruct((PACKED + HALF, half), F32),
            pltpu.VMEM((leaf, 2 * half), BF16),
            pltpu.VMEM((leaf, 2 * half), BF16),
        ),
        grid_spec=pltpu.PrefetchScalarGridSpec(
            num_scalar_prefetch=1, grid=(1,), in_specs=[whole] * 4, out_specs=[whole] * 3
        ),
        input_output_aliases={2: 1, 3: 2},
    )(me, block, high, low, other)


def row_of(x, k):
    return jnp.broadcast_to(x[k : k + 1, :], TILE)


def columns(panel, at):
    return [
        jnp.take_along_axis(panel, jnp.full(TILE, at + m, jnp.int32), axis=1)
        for m in range(ROWS)
    ]


def outer_pieces(a, b):
    a0, a1, a2 = thirds(a)
    b0, b1, b2 = thirds(b)
    left = jnp.concatenate([a0, a0, a1, a0, a1, a2], 0).astype(BF16)
    right = jnp.concatenate([b0, b1, b0, b2, b1, b0], 0).astype(BF16)
    return left, right


def eliminate(panels, nexts, at):
    count = range(len(panels))
    lane = lax.broadcasted_iota(jnp.int32, TILE, 1)
    sub = lax.broadcasted_iota(jnp.int32, TILE, 0)
    here = (lane >= at) & (lane < at + ROWS)
    unit = jnp.where(lane - at == sub, 1.0, 0.0)
    cols = [columns(panels[l], at) for l in count]
    rows = [jnp.where(here, unit, panels[l]) for l in count]
    lows = [jnp.zeros(TILE, F32) for l in count]
    below = [columns(panel, at) for panel in nexts]
    nexts = [jnp.where(here, 0.0, panel) for panel in nexts]
    for k in range(ROWS):
        inv = [lax.rsqrt(row_of(cols[l][k], k)) for l in count]
        low = [jnp.where(sub >= k, cols[l][k] * inv[l], 0.0) for l in count]
        for l in count:
            lead = row_of(rows[l], k) * inv[l]
            rows[l] = jnp.where(sub == k, lead, rows[l] - low[l] * lead)
            lows[l] = jnp.where(lane == at + k, low[l], lows[l])
            if nexts:
                below[l][k] = below[l][k] * inv[l]
                nexts[l] = nexts[l] - below[l][k] * lead
        for m in range(k + 1, ROWS):
            for l in count:
                one = row_of(low[l], m)
                cols[l][m] = cols[l][m] - low[l] * one
                if nexts:
                    below[l][m] = below[l][m] - below[l][k] * one
    return rows, lows, nexts


def factor_block(work, ups, invs, base):
    count = range(work.shape[0])
    lane = lax.broadcasted_iota(jnp.int32, TILE, 1)
    span = slice(base, base + LANES)
    pair = 2 * ROWS
    for at in range(0, LANES, pair):
        mid, end = at + ROWS, at + pair
        both = [work[l, at:end, :] for l in count]
        first, low_first, second = eliminate(
            [b[:ROWS] for b in both], [b[ROWS:] for b in both], at
        )
        second, low_second, _ = eliminate(second, [], mid)
        for l in count:
            for x, low, p in ((first, low_first, at), (second, low_second, mid)):
                to = slice(base + p, base + p + ROWS)
                ups[l, to, span] = jnp.where(lane >= p + ROWS, x[l], low[l])
                invs[l, to, span] = jnp.where(lane < p + ROWS, x[l], 0.0)
        if end == LANES:
            break
        lefts, rights = [], []
        for l in count:
            lefts.append(jnp.concatenate([first[l], second[l]], 0))
            rights.append(
                jnp.concatenate(
                    [jnp.where((lane >= mid) & (lane < end), 0.0, first[l]), second[l]], 0
                )
            )
        pieces = [outer_pieces(lefts[l], rights[l]) for l in count]
        col = lax.broadcasted_iota(jnp.int32, (LANES - end, LANES), 1)
        gone = (col >= at) & (col < end)
        sums = [dot16(pieces[l][0][:, end:], pieces[l][1], 0, 0) for l in count]
        for l in count:
            work[l, end:, :] = jnp.where(gone, 0.0, work[l, end:, :]) - sums[l]


def straighten(ups, l, base):
    n = LANES
    block = ups[l, base : base + n, base : base + n]
    row = lax.broadcasted_iota(jnp.int32, (n, n), 0)
    col = lax.broadcasted_iota(jnp.int32, (n, n), 1)
    ups[l, base : base + n, base : base + n] = jnp.where(row >> 3 == col >> 3, block.T, block)


def factor(grams, work, ups, invs):
    n = LANES
    blank = jnp.zeros((n, n), F32)
    count = range(work.shape[0])
    for l in count:
        work[l] = grams(l, 0)
    factor_block(work, ups, invs, 0)
    sides = [dot(invs[l, 0:n, 0:n], grams(l, 1), 1, 1) for l in count]
    for l in count:
        ups[l, 0:n, n : 2 * n] = sides[l]
        ups[l, n : 2 * n, 0:n] = blank
        invs[l, 0:n, n : 2 * n] = blank
    squares = [dot(sides[l], sides[l], 0, 0) for l in count]
    for l in count:
        work[l] = grams(l, 2) - squares[l]
    factor_block(work, ups, invs, n)
    downs = [dot(ups[l, 0:n, n : 2 * n], invs[l, 0:n, 0:n], 0, 0) for l in count]
    downs = [dot(invs[l, n : 2 * n, n : 2 * n], downs[l], 1, 0) for l in count]
    for l in count:
        invs[l, n : 2 * n, 0:n] = -downs[l]
        straighten(ups, l, 0)
        straighten(ups, l, n)


def factor_kernel(
    me, mine, theirs, highs, lows, transfer, basis, pieces, work, ups, invs, moved, rows, sems
):
    n = LANES
    height = PACKED + HALF
    pieces[me[0]] = mine[...]
    pieces[1 - me[0]] = theirs[...]

    def gram(l, b):
        at = l * height
        if b == 1:
            return jnp.concatenate([pieces[p, at + PACKED : at + height, :] for p in range(2)], 0)
        part = pieces.at[b // 2]
        return unpack(part[at : at + HALF, :], part[at + HALF : at + PACKED, :])

    factor(gram, work, ups, invs)
    cols = pl.ds(pl.multiple_of(me[0] * n, n), n)
    rest = pl.ds(pl.multiple_of((1 - me[0]) * n, n), n)
    scale = math.sqrt(2**LEVELS * highs.shape[0])
    weight = invs.at[LEVELS]
    high, low = halves(jnp.concatenate([weight[cols, cols], weight[cols, rest]], 1) * scale)
    both = jnp.concatenate([high, low], 0)
    steps, size, _ = rows.shape
    copies = []
    for s in range(steps):
        at = slice(s * size, (s + 1) * size)
        two = dot16(highs[at, :], both, 1, 1)
        rows[s] = two[:, :n] + (two[:, n:] + dot16(lows[at, :], high, 1, 1))
        copies.append(pltpu.make_async_copy(rows.at[s], basis.at[pl.ds(s * size, size)], sems.at[s]))
        copies[-1].start()
    for l in range(LEVELS):
        moved[l] = dot(ups[l], invs[l + 1, cols, :], 1, 1)
        copies.append(pltpu.make_async_copy(moved.at[l], transfer.at[l], sems.at[steps + l]))
        copies[-1].start()
    for copy in copies:
        copy.wait()


def factors(me, mine, theirs, highs, lows):
    n = 2 * LANES
    count = LEVELS + 1
    leaf, half = highs.shape[0], LANES
    steps = 6
    whole = pl.BlockSpec(memory_space=pltpu.VMEM)
    return call(
        factor_kernel,
        (
            jax.ShapeDtypeStruct((LEVELS, n, half), F32),
            jax.ShapeDtypeStruct((leaf, half), F32),
        ),
        grid_spec=pltpu.PrefetchScalarGridSpec(
            num_scalar_prefetch=1,
            grid=(1,),
            in_specs=[whole] * 4,
            out_specs=[pl.BlockSpec(memory_space=pl.ANY)] * 2,
            scratch_shapes=[
                pltpu.VMEM((2, *mine.shape), F32),
                pltpu.VMEM((count, LANES, LANES), F32),
                pltpu.VMEM((count, n, n), F32),
                pltpu.VMEM((count, n, n), F32),
                pltpu.VMEM((LEVELS, n, half), F32),
                pltpu.VMEM((steps, leaf // steps, half), F32),
                pltpu.SemaphoreType.DMA((steps + LEVELS,)),
            ],
        ),
    )(me, mine, theirs, highs, lows)


def beside(array, shift):
    count = lax.axis_size("leaf")
    pairs = [(i, i + shift) for i in range(count) if 0 <= i + shift < count]
    return lax.ppermute(array, "leaf", pairs)


def sibling(array, flip):
    return lax.ppermute(array, "leaf", [(i, i ^ flip) for i in range(lax.axis_size("leaf"))])


def other_core(array):
    return lax.ppermute(array, "probe", [(0, 1), (1, 0)])


def body(features, probes, lengthscale, near_blocks, leaf_order):
    blocks = near_blocks.shape[0]
    me = lax.axis_index("probe").astype(jnp.int32)[None]
    first = ((lax.axis_index("leaf") - 1) * blocks).astype(jnp.int32)[None]
    stack = order_features(features, leaf_order, probes)
    before = beside(stack, 1)
    after = beside(stack, -1)
    part, rows_t, far, weight = near_part(near_blocks, first, lengthscale, stack, probes)
    own = far_part(far, weight, part, rows_t, before, after, blocks)
    other = other_core(own)
    block, high, low = own_gram(own)
    gram, highs, lows = gram_blocks(me, block, high, low, other)
    grams = [gram]
    for flip in (1, 2, 7, 8):
        gram = gram + sibling(gram, flip)
        grams.append(gram)
    mine = jnp.concatenate(grams, 0)
    return factors(me, mine, other_core(mine), highs, lows)


def solution(mesh):
    in_specs = (P(None, "leaf"), P("probe", "leaf"), P(), P("leaf", None), P("leaf", None))
    out_specs = (P(None, "leaf", "probe"), P("leaf", "probe"))
    return jax.shard_map(body, mesh=mesh, in_specs=in_specs, out_specs=out_specs, check_vma=False)
```
